128 devices in a mesh: dp: 16 (over x_lo, z, core), chan: 8 (over y, x_hi).
Axes of the slice: x: 4 (x_hi: 2, x_lo: 2; x = x_hi * 2 + x_lo), y: 4, z: 4, core: 2. Of those that a mesh axis runs over, the one named last changes fastest.
Arguments:
- volume: bfloat16 [16, 512, 1024], P('dp', 'chan'), may hold values from -16 to 16
- w_first: bfloat16 [27, 512, 512], P(None, 'chan'), may hold values from -0.0546875 to 0.0546875
- gain: float32 [512], replicated, may hold values from 0.1 to 1.9
- w_second: bfloat16 [27, 512, 512], P(None, None, 'chan'), may hold values from -0.0546875 to 0.0546875
- cotangent: bfloat16 [16, 512, 1024], P('dp', 'chan'), may hold values from -8 to 8
Outputs:
- output: bfloat16 [16, 512, 1024], P('dp', 'chan')
- grad_volume: bfloat16 [16, 512, 1024], P('dp', 'chan')
- grad_w_first: float32 [27, 512, 512], P(None, 'chan')
- grad_gain: float32 [512], P('chan')
- grad_w_second: float32 [27, 512, 512], P(None, None, 'chan')
The draws below stay inside these ranges and needn't reach their ends.
All inputs are finite; a program needn't handle non-finite values.
Results may differ from the reference program's by a relative error of at most 0.005.
Values may be sent and summed in bfloat16 or wider, within the bound.
A program may use at most 64 MiB of HBM per device.

```python
import math
import jax
import jax.numpy as jnp
from jax import lax

CHANNELS = 512
DEPTH = 4
HEIGHT = 16
WIDTH = 16
VOXELS = 1024
SUBVOLUMES = 16


def draw_volume(key, part):
    subkeys = jax.random.split(key, 3)
    shape_all = (SUBVOLUMES, CHANNELS, VOXELS)
    chan_scale = jnp.exp(jax.random.uniform(subkeys[0], (1, CHANNELS, 1), jnp.float32, 0.0, 1.0) * (0.5 * math.log(10.0)))
    cell_scale = jnp.exp(jax.random.uniform(subkeys[1], (SUBVOLUMES, 1, VOXELS), jnp.float32, 0.0, 1.0) * (0.5 * math.log(10.0)))
    shrink = 1.0 / math.sqrt(10.0)
    entries = jnp.clip(jax.random.normal(subkeys[2], shape_all, jnp.float32), -5.0, 5.0)
    field = entries * chan_scale * cell_scale * shrink
    return field.astype(jnp.bfloat16)


def draw_cotangent(key, part):
    subkeys = jax.random.split(key, 1)
    shape_all = (SUBVOLUMES, CHANNELS, VOXELS)
    growth = 1.0 + 2.0 * jnp.arange(SUBVOLUMES, dtype=jnp.float32)[:, None, None] / max(SUBVOLUMES - 1, 1)
    entries = jnp.clip(jax.random.normal(subkeys[0], shape_all, jnp.float32), -5.0, 5.0)
    field = entries * growth * 0.5
    return field.astype(jnp.bfloat16)


def block_scale(stream_key, dims, shards, smallest, largest):
    level, own = 1.0, jax.random.fold_in(stream_key, 6)
    for axis_at, blocks in shards:
        heights = jnp.exp(jax.random.uniform(jax.random.fold_in(own, axis_at), (blocks,), jnp.float32, smallest / len(shards), largest / len(shards)))
        level = level * jnp.repeat(heights, dims[axis_at] // blocks).reshape([-1 if axis == axis_at else 1 for axis in range(len(dims))])
    return level


def bell_draw(own_key, extent, scale, most, cuts=(), kind=jnp.bfloat16):
    values = jax.random.normal(own_key, extent, jnp.float32) * scale
    if len(cuts) > 0:
        values = block_scale(own_key, extent, cuts, -0.22, 0.18) * values
    return jnp.clip(values, min=-most, max=most).astype(kind)


def setup_inputs(seed: int = 0) -> dict:
    keys = jax.random.split(jax.random.key(seed), 6)
    return {
        "volume": draw_volume(jax.random.fold_in(keys[5], 71), 0),
        "w_first": bell_draw(keys[1], (27, CHANNELS, CHANNELS), (27 * CHANNELS) ** -0.5, 0.0546875, ((1, 8),)),
        "gain": jnp.clip(1.0 + 0.18 * jax.random.normal(keys[2], (CHANNELS,), jnp.float32), 0.1, 1.9),
        "w_second": bell_draw(keys[3], (27, CHANNELS, CHANNELS), (27 * CHANNELS) ** -0.5, 0.0546875, ((2, 8),)),
        "cotangent": draw_cotangent(jax.random.fold_in(keys[5], 71), 0),
    }


TAP_OFFSETS = [(plane_off, row_off, col_off) for plane_off in (-1, 0, 1) for row_off in (-1, 0, 1) for col_off in (-1, 0, 1)]
NORM_EPS = 1e-05

def shifted(field, plane_off, row_off, col_off):
    shaped = field.reshape(field.shape[0], field.shape[1], DEPTH, HEIGHT, WIDTH)
    padded = jnp.pad(shaped, ((0, 0), (0, 0), (1, 1), (1, 1), (1, 1)))
    window = padded[:, :, 1 + plane_off:1 + plane_off + DEPTH, 1 + row_off:1 + row_off + HEIGHT, 1 + col_off:1 + col_off + WIDTH]
    return window.reshape(field.shape)

def forward_conv(field, weights):
    result = jnp.zeros((field.shape[0], weights.shape[2], field.shape[2]), jnp.float32)
    for index, offsets in enumerate(TAP_OFFSETS):
        moved = shifted(field, offsets[0], offsets[1], offsets[2]).astype(jnp.float32)
        result = result + jnp.einsum('bcp,cf->bfp', moved, weights[index].astype(jnp.float32))
    return result

def backward_conv(field, weights):
    result = jnp.zeros((field.shape[0], weights.shape[1], field.shape[2]), jnp.float32)
    for index, offsets in enumerate(TAP_OFFSETS):
        moved = shifted(field, -offsets[0], -offsets[1], -offsets[2]).astype(jnp.float32)
        result = result + jnp.einsum('bfp,cf->bcp', moved, weights[index].astype(jnp.float32))
    return result

def weight_grad(field, other):
    other_wide = other.astype(jnp.float32)
    layers = []
    for offsets in TAP_OFFSETS:
        moved = shifted(field, offsets[0], offsets[1], offsets[2]).astype(jnp.float32)
        layers.append(jnp.einsum('bcp,bfp->cf', moved, other_wide))
    return jnp.stack(layers, axis=0)

def reference(volume, w_first, gain, w_second, cotangent):
    pre = forward_conv(volume, w_first)
    center = pre - lax.optimization_barrier(jnp.mean(pre, axis=2, keepdims=True))
    inverse = lax.rsqrt(lax.optimization_barrier(jnp.mean(center * center, axis=2, keepdims=True)) + NORM_EPS)
    normed = center * inverse
    gain_wide = gain.astype(jnp.float32)[None, :, None]
    scaled = gain_wide * normed
    act = jax.nn.silu(scaled).astype(jnp.bfloat16)
    output = forward_conv(act, w_second).astype(jnp.bfloat16)
    factor = 1.0 / math.sqrt(SUBVOLUMES * VOXELS)
    dact = backward_conv(cotangent, w_second)
    grad_w_second = weight_grad(act, cotangent) * factor
    sigma = jax.nn.sigmoid(scaled)
    dscaled = dact * sigma * (1.0 + scaled * (1.0 - sigma))
    grad_gain = lax.optimization_barrier(jnp.sum(dscaled * normed, axis=(0, 2))) * factor
    dnormed = dscaled * gain_wide
    dpre = ((dnormed - lax.optimization_barrier(jnp.mean(dnormed, axis=2, keepdims=True)) - normed * lax.optimization_barrier(jnp.mean(dnormed * normed, axis=2, keepdims=True))) * inverse).astype(jnp.bfloat16)
    grad_volume = backward_conv(dpre, w_first).astype(jnp.bfloat16)
    grad_w_first = weight_grad(volume, dpre) * factor
    return (output, grad_volume, grad_w_first, grad_gain, grad_w_second)
```

```python
import math

import jax
import jax.numpy as jnp
from jax import lax
from jax.experimental import pallas as pl
from jax.experimental.pallas import tpu as pltpu
from jax.sharding import PartitionSpec as P

NORM_EPS = 1e-05
PLANES, ROWS, COLS = 4, 16, 16
PLANE = ROWS * COLS
CELLS = PLANES * PLANE
OWN = 64
ALL = 512
TAPS = 27
TALL = TAPS * OWN
ZBLOCK = TALL // 4
HALF = ALL // 2
QUART = ALL // 4
MESH = pl.DeviceIdType.MESH
F32 = jnp.float32
BF16 = jnp.bfloat16


def inside(shape, row_off, col_off):
    cell = lax.broadcasted_iota(jnp.int32, shape, 1)
    row = cell // COLS % ROWS + row_off
    col = cell % COLS + col_off
    return (row >= 0) & (row < ROWS) & (col >= 0) & (col < COLS)


def moved(field, row_off, col_off):
    offset = row_off * COLS + col_off
    if offset == 0:
        return field
    rolled = pltpu.roll(field, (-offset) % CELLS, axis=1)
    return jnp.where(inside(field.shape, row_off, col_off), rolled, 0.0)


def build_columns(src, dst, sign):
    field = src[...].astype(F32)
    blank = jnp.zeros((OWN, PLANE), BF16)
    for b in (-1, 0, 1):
        for c in (-1, 0, 1):
            block = moved(field, sign * b, sign * c).astype(BF16)
            for a in (-1, 0, 1):
                tap = 9 * (a + 1) + 3 * (b + 1) + c + 1
                rows = pl.ds(tap * OWN, OWN)
                step = sign * a
                if step == 0:
                    dst[rows, :] = block
                elif step > 0:
                    dst[rows, 0 : CELLS - PLANE] = block[:, PLANE:]
                    dst[rows, CELLS - PLANE : CELLS] = blank
                else:
                    dst[rows, PLANE:CELLS] = block[:, : CELLS - PLANE]
                    dst[rows, 0:PLANE] = blank


def turn(src, dst):
    def one(index, carry):
        at = pl.multiple_of(index * 128, 128)
        dst[:, pl.ds(at, 128)] = src[pl.ds(at, 128), :].T
        return carry

    lax.fori_loop(0, TALL // 128, one, 0)
    rest = TALL // 128 * 128
    dst[:, rest:TALL] = src[rest:TALL, :].T


def partial_sums(turned, columns, dst, first, last):
    def one(index, carry):
        at = pl.multiple_of(index * PLANE, PLANE)
        dst[:, pl.ds(at, PLANE)] = jnp.dot(
            turned[...], columns[:, pl.ds(at, PLANE)], preferred_element_type=F32
        ).astype(BF16)
        return carry

    lax.fori_loop(first, last, one, 0)


def conv_out(weights, gathered, wide, dst, sign):
    nine = 9 * OWN
    for d in range(PLANES):
        total = None
        for a in (-1, 0, 1):
            plane = d + sign * a
            if plane < 0 or plane >= PLANES:
                continue
            term = jnp.dot(
                weights[pl.ds((a + 1) * nine, nine), :],
                gathered[:, pl.ds(plane * PLANE, PLANE)],
                preferred_element_type=F32,
            )
            total = term if total is None else total + term
        wide[:, pl.ds(d * PLANE, PLANE)] = total

    def one(index, carry):
        at = pl.multiple_of(index * 16, 16)
        total = jnp.zeros((16, CELLS), F32)
        for b in (-1, 0, 1):
            for c in (-1, 0, 1):
                tap = 3 * (b + 1) + c + 1
                total = total + moved(wide[pl.ds(tap * OWN + at, 16), :], sign * b, sign * c)
        dst[pl.ds(at, 16), :] = total.astype(BF16)
        return carry

    lax.fori_loop(0, OWN // 16, one, 0)


def kernel(
    volume, w_first, gain, w_second, cotangent,
    output, grad_volume, grad_first, grad_gain, grad_second,
    vol_cols, cot_cols, turned, sums_a, sums_b, got_a, got_b, act, dpre,
    normed, sigma, inverse, wide,
    core_out_a, core_in_a, z_out_a, z_in_a, keep_a, x_out_a, x_in_a,
    core_out_b, core_in_b, z_out_b, z_in_b, keep_b, x_out_b, x_in_b,
    gain_core, gain_z, gain_x, send_sems, recv_sems,
):
    dp = lax.axis_index("dp")
    chan = lax.axis_index("chan")
    x_lo, z, core = dp // 8, dp // 2 % 4, dp % 2
    y, x_hi = chan // 2, chan % 2
    count = [0]

    def send(src, dst, device):
        index = count[0]
        count[0] += 1
        copy = pltpu.make_async_remote_copy(
            src_ref=src,
            dst_ref=dst,
            send_sem=send_sems.at[index],
            recv_sem=recv_sems.at[index],
            device_id=device,
            device_id_type=MESH,
        )
        copy.start()
        pending.append(copy)
        return copy

    pending = []
    peers = []
    for k in (4, 2, 6, 1, 5, 3, 7):
        other = (y + k // 2) % 4 * 2 + (x_hi + k % 2) % 2
        peers.append((other, (dp, other)))
    core_peer = (x_lo * 8 + z * 2 + 1 - core, chan)
    x_peer = ((1 - x_lo) * 8 + z * 2 + core, chan)
    z_peer = {j: (x_lo * 8 + (z + j) % 4 * 2 + core, chan) for j in (1, 2, 3)}

    barrier = pltpu.get_barrier_semaphore()
    everyone = [device for _, device in peers] + [core_peer, x_peer] + list(z_peer.values())
    for device in everyone:
        pl.semaphore_signal(barrier, inc=1, device_id=device, device_id_type=MESH)

    def scatter(sums, got, first, width):
        copies = []
        cells = pl.ds(first, width)
        for slot, (other, device) in enumerate(peers):
            rows = pl.ds(pl.multiple_of(other * OWN, OWN), OWN)
            copies.append(send(sums.at[rows, cells], got.at[slot, :, cells], device))
        return copies

    def share(block):
        rows = pl.ds(pl.multiple_of(chan * OWN, OWN), OWN)
        return [send(block.at[rows, :], block.at[rows, :], device) for _, device in peers]

    def arrived(copies):
        for copy in copies:
            copy.wait_recv()

    build_columns(volume, vol_cols, 1)
    turn(w_first, turned)
    partial_sums(turned, vol_cols, sums_a, 0, 2)
    pl.semaphore_wait(barrier, len(everyone))
    first_sums = scatter(sums_a, got_a, 0, CELLS // 2)
    partial_sums(turned, vol_cols, sums_a, 2, 4)
    first_sums += scatter(sums_a, got_a, CELLS // 2, CELLS // 2)

    build_columns(cotangent, cot_cols, -1)
    turn(w_second, turned)
    partial_sums(turned, cot_cols, sums_b, 0, 2)
    second_sums = scatter(sums_b, got_b, 0, CELLS // 2)
    partial_sums(turned, cot_cols, sums_b, 2, 4)

    place = lax.broadcasted_iota(jnp.int32, (OWN, ALL), 1)
    wanted = lax.broadcasted_iota(jnp.int32, (OWN, ALL), 0) + chan * OWN
    gain_own = jnp.sum(
        jnp.where(place == wanted, jnp.broadcast_to(gain[...], (OWN, ALL)), 0.0),
        axis=1,
        keepdims=True,
    )
    scale = 1.0 / CELLS

    def summed(sums, got, at):
        total = sums[pl.ds(pl.multiple_of(chan * OWN + at, 16), 16), :].astype(F32)
        for slot in range(7):
            total = total + got[slot, pl.ds(at, 16), :].astype(F32)
        return total

    arrived(first_sums)
    for group in range(OWN // 16):
        at = group * 16
        gain_rows = gain_own[at : at + 16]
        pre = summed(sums_a, got_a, at)
        center = pre - jnp.sum(pre, axis=1, keepdims=True) * scale
        inv = lax.rsqrt(jnp.sum(center * center, axis=1, keepdims=True) * scale + NORM_EPS)
        unit = center * inv
        scaled = gain_rows * unit
        sig = jax.nn.sigmoid(scaled)
        normed[pl.ds(at, 16), :] = unit
        sigma[pl.ds(at, 16), :] = sig
        inverse[pl.ds(at, 16), :] = jnp.broadcast_to(inv, (16, 128))
        act[pl.ds(pl.multiple_of(chan * OWN + at, 16), 16), :] = (scaled * sig).astype(BF16)
    act_copies = share(act)
    second_sums += scatter(sums_b, got_b, CELLS // 2, CELLS // 2)

    arrived(second_sums)
    gain_row = jnp.zeros((8, 128), F32)
    for group in range(OWN // 16):
        at = group * 16
        gain_rows = gain_own[at : at + 16]
        dact = summed(sums_b, got_b, at)
        unit = normed[pl.ds(at, 16), :]
        sig = sigma[pl.ds(at, 16), :]
        inv = inverse[pl.ds(at, 16), 0:1]
        scaled = gain_rows * unit
        dscaled = dact * sig * (1.0 + scaled * (1.0 - sig))
        part = jnp.sum(dscaled * unit, axis=1, keepdims=True)
        spot = lax.broadcasted_iota(jnp.int32, (16, 128), 1)
        here = lax.broadcasted_iota(jnp.int32, (16, 128), 0) + at
        row = jnp.sum(jnp.where(spot == here, part, 0.0), axis=0, keepdims=True)
        gain_row = gain_row + jnp.broadcast_to(row, (8, 128))
        dnormed = dscaled * gain_rows
        mean_d = jnp.sum(dnormed, axis=1, keepdims=True) * scale
        mean_u = jnp.sum(dnormed * unit, axis=1, keepdims=True) * scale
        back = (dnormed - mean_d - unit * mean_u) * inv
        dpre[pl.ds(pl.multiple_of(chan * OWN + at, 16), 16), :] = back.astype(BF16)
    dpre_copies = share(dpre)
    gain_core[0] = gain_row
    gain_core_copy = send(gain_core.at[0], gain_core.at[1], core_peer)

    order = (2, 1, 3, 0)

    def z_rows(j):
        return pl.ds(pl.multiple_of((z + j) % 4 * ZBLOCK, ZBLOCK), ZBLOCK)

    def against(columns, gathered, rows, side):
        half = gathered[pl.ds(pl.multiple_of(side * HALF, HALF), HALF), :]
        return lax.dot_general(
            columns[rows, :], half, (((1,), (1,)), ((), ())), preferred_element_type=F32
        )

    def reduce_start(columns, gathered, core_out, core_in, z_out, z_in, keep):
        crossing = {}
        for j in order:
            core_out[j] = against(columns, gathered, z_rows(j), 1 - core).astype(BF16)
            crossing[j] = send(core_out.at[j], core_in.at[j], core_peer)
        z_copies = []
        for j in order:
            mine = against(columns, gathered, z_rows(j), core)
            crossing[j].wait_recv()
            mine = mine + core_in[j].astype(F32)
            if j == 0:
                keep[...] = mine
            else:
                z_out[j - 1] = mine.astype(BF16)
                z_copies.append(send(z_out.at[j - 1], z_in.at[j - 1], z_peer[j]))
        return z_copies

    def lanes(side):
        return pl.ds(pl.multiple_of(side * QUART, QUART), QUART)

    def reduce_x(z_copies, z_in, keep, x_out, x_in):
        arrived(z_copies)
        keep[...] = keep[...] + z_in[0].astype(F32) + z_in[1].astype(F32) + z_in[2].astype(F32)
        x_out[...] = keep[:, lanes(1 - x_lo)].astype(BF16)
        return send(x_out, x_in, x_peer)

    factor = 1.0 / math.sqrt(lax.axis_size("dp") * CELLS)

    def spread_x(x_copy, keep, x_in, final):
        x_copy.wait_recv()
        rows = z_rows(0)
        mine = lanes(core * 2 + x_lo)
        final[rows, mine] = ((keep[:, lanes(x_lo)] + x_in[...].astype(F32)) * factor).astype(BF16)
        spot = final.at[rows, mine]
        to_x = send(spot, spot, x_peer)
        return to_x, {j: [send(spot, spot, z_peer[j])] for j in (2, 1, 3)}

    def spread_z(spread, final):
        to_x, to_z = spread
        to_x.wait_recv()
        rows = z_rows(0)
        spot = final.at[rows, lanes(core * 2 + 1 - x_lo)]
        for j in (2, 1, 3):
            to_z[j].append(send(spot, spot, z_peer[j]))
        whole = final.at[rows, pl.ds(pl.multiple_of(core * HALF, HALF), HALF)]
        return to_z, [send(whole, whole, core_peer)]

    def spread_core(state, final):
        to_z, to_core = state
        for j in (1, 3, 2):
            arrived(to_z[j])
            whole = final.at[z_rows(4 - j), pl.ds(pl.multiple_of(core * HALF, HALF), HALF)]
            to_core.append(send(whole, whole, core_peer))
        return to_core

    arrived(act_copies)
    z_second = reduce_start(cot_cols, act, core_out_b, core_in_b, z_out_b, z_in_b, keep_b)
    conv_out(w_second, act, wide, output, 1)

    arrived(dpre_copies)
    gain_core_copy.wait_recv()
    gain_mine = gain_core[0] + gain_core[1]
    gain_z[z] = gain_mine
    gain_copies = [send(gain_z.at[z], gain_z.at[z], z_peer[j]) for j in (1, 2, 3)]
    z_first = reduce_start(vol_cols, dpre, core_out_a, core_in_a, z_out_a, z_in_a, keep_a)

    x_second = reduce_x(z_second, z_in_b, keep_b, x_out_b, x_in_b)
    arrived(gain_copies)
    gain_x[0] = (gain_z[0] + gain_z[1]) + (gain_z[2] + gain_z[3])
    gain_x_copy = send(gain_x.at[0], gain_x.at[1], x_peer)
    second_spread = spread_x(x_second, keep_b, x_in_b, grad_second)
    second_state = spread_z(second_spread, grad_second)
    conv_out(w_first, dpre, wide, grad_volume, -1)
    x_first = reduce_x(z_first, z_in_a, keep_a, x_out_a, x_in_a)
    first_spread = spread_x(x_first, keep_a, x_in_a, grad_first)
    first_state = spread_z(first_spread, grad_first)
    last = spread_core(second_state, grad_second)
    gain_x_copy.wait_recv()
    grad_gain[...] = (gain_x[0] + gain_x[1]) * factor
    last += spread_core(first_state, grad_first)
    arrived(last)
    for copy in pending:
        copy.wait_send()


def shards(volume, w_first, gain, w_second, cotangent):
    vmem = pl.BlockSpec(memory_space=pltpu.VMEM)
    shape = jax.ShapeDtypeStruct
    reducing = [
        pltpu.VMEM((4, ZBLOCK, HALF), BF16),
        pltpu.VMEM((4, ZBLOCK, HALF), BF16),
        pltpu.VMEM((3, ZBLOCK, HALF), BF16),
        pltpu.VMEM((3, ZBLOCK, HALF), BF16),
        pltpu.VMEM((ZBLOCK, HALF), F32),
        pltpu.VMEM((ZBLOCK, QUART), BF16),
        pltpu.VMEM((ZBLOCK, QUART), BF16),
    ]
    output, grad_volume, grad_first, grad_gain, grad_second = pl.pallas_call(
        kernel,
        name="conv_pair",
        out_shape=(
            shape((OWN, CELLS), BF16),
            shape((OWN, CELLS), BF16),
            shape((TALL, ALL), BF16),
            shape((8, 128), F32),
            shape((TALL, ALL), BF16),
        ),
        in_specs=[vmem] * 5,
        out_specs=[vmem] * 5,
        scratch_shapes=[
            pltpu.VMEM((TALL, CELLS), BF16),
            pltpu.VMEM((TALL, CELLS), BF16),
            pltpu.VMEM((ALL, TALL), BF16),
            pltpu.VMEM((ALL, CELLS), BF16),
            pltpu.VMEM((ALL, CELLS), BF16),
            pltpu.VMEM((7, OWN, CELLS), BF16),
            pltpu.VMEM((7, OWN, CELLS), BF16),
            pltpu.VMEM((ALL, CELLS), BF16),
            pltpu.VMEM((ALL, CELLS), BF16),
            pltpu.VMEM((OWN, CELLS), F32),
            pltpu.VMEM((OWN, CELLS), F32),
            pltpu.VMEM((OWN, 128), F32),
            pltpu.VMEM((9 * OWN, CELLS), F32),
        ]
        + reducing
        + reducing
        + [
            pltpu.VMEM((2, 8, 128), F32),
            pltpu.VMEM((4, 8, 128), F32),
            pltpu.VMEM((2, 8, 128), F32),
            pltpu.SemaphoreType.DMA((96,)),
            pltpu.SemaphoreType.DMA((96,)),
        ],
        compiler_params=pltpu.CompilerParams(
            collective_id=0, has_side_effects=True, vmem_limit_bytes=60 << 20
        ),
    )(
        volume[0],
        w_first.reshape(TALL, ALL),
        gain.reshape(1, ALL),
        w_second.transpose(0, 2, 1).reshape(TALL, ALL),
        cotangent[0],
    )
    return (
        output[None],
        grad_volume[None],
        grad_first.astype(F32).reshape(TAPS, OWN, ALL),
        grad_gain[0, :OWN],
        grad_second.astype(F32).reshape(TAPS, OWN, ALL).transpose(0, 2, 1),
    )


def solution(mesh):
    placed = (
        P("dp", "chan", None),
        P(None, "chan", None),
        P(),
        P(None, None, "chan"),
        P("dp", "chan", None),
    )
    return jax.shard_map(
        shards,
        mesh=mesh,
        in_specs=placed,
        out_specs=(
            P("dp", "chan", None),
            P("dp", "chan", None),
            P(None, "chan", None),
            P("chan"),
            P(None, None, "chan"),
        ),
        check_vma=False,
    )
```

```python
import math

import jax
import jax.numpy as jnp
from jax import lax
from jax.experimental import pallas as pl
from jax.experimental.pallas import tpu as pltpu
from jax.sharding import PartitionSpec as P

NORM_EPS = 1e-05
PLANES, ROWS, COLS = 4, 16, 16
PLANE = ROWS * COLS
CELLS = PLANES * PLANE
OWN = 64
ALL = 512
TAPS = 27
TALL = TAPS * OWN
ZBLOCK = TALL // 4
HALF = ALL // 2
QUART = ALL // 4
RUN = 32
MESH = pl.DeviceIdType.MESH
F32 = jnp.float32
BF16 = jnp.bfloat16


def inside(shape, row_off, col_off):
    cell = lax.broadcasted_iota(jnp.int32, shape, 1)
    row = cell // COLS % ROWS + row_off
    col = cell % COLS + col_off
    return (row >= 0) & (row < ROWS) & (col >= 0) & (col < COLS)


def moved(field, row_off, col_off):
    offset = row_off * COLS + col_off
    if offset == 0:
        return field
    rolled = pltpu.roll(field, (-offset) % CELLS, axis=1)
    return jnp.where(inside(field.shape, row_off, col_off), rolled, 0.0)


def build_columns(src, dst, sign):
    field = src[...].astype(F32)
    blank = jnp.zeros((OWN, PLANE), BF16)
    for b in (-1, 0, 1):
        for c in (-1, 0, 1):
            block = moved(field, sign * b, sign * c).astype(BF16)
            for a in (-1, 0, 1):
                tap = 9 * (a + 1) + 3 * (b + 1) + c + 1
                rows = pl.ds(tap * OWN, OWN)
                step = sign * a
                if step == 0:
                    dst[rows, :] = block
                elif step > 0:
                    dst[rows, 0 : CELLS - PLANE] = block[:, PLANE:]
                    dst[rows, CELLS - PLANE : CELLS] = blank
                else:
                    dst[rows, PLANE:CELLS] = block[:, : CELLS - PLANE]
                    dst[rows, 0:PLANE] = blank


def turn(src, dst):
    def one(index, carry):
        at = pl.multiple_of(index * 128, 128)
        dst[:, pl.ds(at, 128)] = src[pl.ds(at, 128), :].T
        return carry

    lax.fori_loop(0, TALL // 128, one, 0)
    rest = TALL // 128 * 128
    dst[:, rest:TALL] = src[rest:TALL, :].T


def partial_sums(turned, columns, wide, dst, first, last):
    def one(index, carry):
        at = pl.multiple_of(index * PLANE, PLANE)
        total = jnp.dot(turned[...], columns[:, pl.ds(at, PLANE)], preferred_element_type=F32)
        total = total.reshape(2, 4, 2, RUN, PLANE)
        wide[:, :, :, :, pl.ds(at, PLANE)] = total
        dst[:, :, :, :, pl.ds(at, PLANE)] = total.astype(BF16)
        return carry

    lax.fori_loop(first, last, one, 0)


def conv_out(weights, gathered, wide, dst, sign):
    nine = 9 * OWN
    for d in range(PLANES):
        total = None
        for a in (-1, 0, 1):
            plane = d + sign * a
            if plane < 0 or plane >= PLANES:
                continue
            term = jnp.dot(
                weights[pl.ds((a + 1) * nine, nine), :],
                gathered[:, :, :, :, pl.ds(plane * PLANE, PLANE)].reshape(ALL, PLANE),
                preferred_element_type=F32,
            )
            total = term if total is None else total + term
        wide[:, pl.ds(d * PLANE, PLANE)] = total

    def one(index, carry):
        at = pl.multiple_of(index * 16, 16)
        total = jnp.zeros((16, CELLS), F32)
        for b in (-1, 0, 1):
            for c in (-1, 0, 1):
                tap = 3 * (b + 1) + c + 1
                total = total + moved(wide[pl.ds(tap * OWN + at, 16), :], sign * b, sign * c)
        dst[pl.ds(at, 16), :] = total.astype(BF16)
        return carry

    lax.fori_loop(0, OWN // 16, one, 0)


def kernel(
    volume_in, w_first_in, gain_in, w_second_in, cotangent_in,
    output_to, grad_volume_to, grad_first_to, grad_gain_to, grad_second_to,
    volume, w_first, w_second, cotangent, output, grad_volume, grad_first, grad_second,
    gain, grad_gain, vol_cols, cot_cols, turned, act, dpre,
    sums_a, wide_a, y_in_a, x_send_a, x_recv_a, x_in_a, y_send_a, y_recv_a, kept_a,
    sums_b, wide_b, y_in_b, x_send_b, x_recv_b, x_in_b, y_send_b, y_recv_b, kept_b,
    normed, sigma, inverse, wide,
    product, core_out, core_in, z_out, z_in, keep, x_out, x_in,
    gain_all, gain_core, gain_z, gain_x, send_sems, recv_sems, own_sems,
):
    dp = lax.axis_index("dp")
    chan = lax.axis_index("chan")
    x_lo, z, core = dp // 8, dp // 2 % 4, dp % 2
    y, x_hi = chan // 2, chan % 2
    pending = []
    moves = []

    def move(src, dst):
        copy = pltpu.make_async_copy(src, dst, own_sems.at[len(moves)])
        copy.start()
        moves.append(copy)
        return copy

    load_volume = move(volume_in, volume)
    load_first = move(w_first_in, w_first)
    load_cotangent = move(cotangent_in, cotangent)
    load_second = move(w_second_in, w_second)
    load_gain = move(gain_in, gain)

    def send(src, dst, device):
        index = len(pending)
        copy = pltpu.make_async_remote_copy(
            src_ref=src,
            dst_ref=dst,
            send_sem=send_sems.at[index],
            recv_sem=recv_sems.at[index],
            device_id=device,
            device_id_type=MESH,
        )
        copy.start()
        pending.append(copy)
        return copy

    peers = []
    for k in (4, 2, 6, 1, 5, 3, 7):
        other = (y + k // 2) % 4 * 2 + (x_hi + k % 2) % 2
        peers.append((other, (dp, other)))
    core_peer = (x_lo * 8 + z * 2 + 1 - core, chan)
    chan_x = (dp, y * 2 + 1 - x_hi)
    chan_y = {j: (dp, (y + j) % 4 * 2 + x_hi) for j in (1, 2, 3)}
    x_peer = ((1 - x_lo) * 8 + z * 2 + core, chan)
    z_peer = {j: (x_lo * 8 + (z + j) % 4 * 2 + core, chan) for j in (1, 2, 3)}

    barrier = pltpu.get_barrier_semaphore()
    everyone = [device for _, device in peers] + [core_peer, x_peer] + list(z_peer.values())
    for device in everyone:
        pl.semaphore_signal(barrier, inc=1, device_id=device, device_id_type=MESH)

    group_a = (sums_a, wide_a, y_in_a, x_send_a, x_recv_a, x_in_a, y_send_a, y_recv_a, kept_a)
    group_b = (sums_b, wide_b, y_in_b, x_send_b, x_recv_b, x_in_b, y_send_b, y_recv_b, kept_b)
    turns = (2, 1, 3)

    def scatter(group, half):
        sums, _, y_in, _, _, x_in, _, _, _ = group
        cells = pl.ds(half * (CELLS // 2), CELLS // 2)
        copies = [send(sums.at[1, :, 1 - x_hi, :, cells], x_in.at[:, :, cells], chan_x)]
        for j in turns:
            spot = sums.at[0, (y + j) % 4, :, :, cells]
            copies.append(send(spot, y_in.at[j - 1, :, :, cells], chan_y[j]))
        return copies

    def scatter_on(group, half, copies):
        _, wide, y_in, x_send, x_recv, x_in, y_send, y_recv, kept = group
        cells = pl.ds(half * (CELLS // 2), CELLS // 2)
        arrived(copies)

        def crossed(side):
            total = wide[0, y, side, :, cells]
            for slot in range(3):
                total = total + y_in[slot, side, :, cells].astype(F32)
            return total

        def along(j):
            row = (y + j) % 4
            return wide[1, row, x_hi, :, cells] + x_in[row, :, cells].astype(F32)

        x_send[:, cells] = crossed(1 - x_hi).astype(BF16)
        later = [send(x_send.at[:, cells], x_recv.at[:, cells], chan_x)]
        for j in turns:
            y_send[j - 1, :, cells] = along(j).astype(BF16)
            later.append(send(y_send.at[j - 1, :, cells], y_recv.at[j - 1, :, cells], chan_y[j]))
        kept[0, :, cells] = crossed(x_hi)
        kept[1, :, cells] = along(0)
        return later

    def share(block):
        own_first = block.at[0, y, x_hi]
        own_second = block.at[1, y, x_hi]
        across = send(own_second, own_second, chan_x)
        along = {j: send(own_first, own_first, chan_y[j]) for j in turns}
        return across, along, [send(own_first, own_first, chan_x)]

    def share_on(block, state):
        across, along, first = state
        across.wait_recv()
        pair = block.at[1, y]
        second = [send(pair, pair, chan_y[j]) for j in turns]
        for j in (1, 3, 2):
            along[j].wait_recv()
            spot = block.at[0, (y + 4 - j) % 4, x_hi]
            first.append(send(spot, spot, chan_x))
        return first, second

    def arrived(copies):
        for copy in copies:
            copy.wait_recv()

    load_volume.wait()
    build_columns(volume, vol_cols, 1)
    load_first.wait()
    turn(w_first, turned)
    partial_sums(turned, vol_cols, wide_a, sums_a, 0, 2)
    pl.semaphore_wait(barrier, len(everyone))
    first_low = scatter(group_a, 0)
    partial_sums(turned, vol_cols, wide_a, sums_a, 2, 4)
    first_high = scatter(group_a, 1)

    load_cotangent.wait()
    build_columns(cotangent, cot_cols, -1)
    load_second.wait()
    turn(w_second, turned)
    first_low = scatter_on(group_a, 0, first_low)
    partial_sums(turned, cot_cols, wide_b, sums_b, 0, 2)
    first_high = scatter_on(group_a, 1, first_high)
    second_low = scatter(group_b, 0)
    partial_sums(turned, cot_cols, wide_b, sums_b, 2, 4)

    load_gain.wait()
    own_row = lax.broadcasted_iota(jnp.int32, (OWN, ALL), 0)
    wanted = own_row // RUN * HALF + chan * RUN + own_row % RUN
    gain_own = jnp.sum(
        jnp.where(
            lax.broadcasted_iota(jnp.int32, (OWN, ALL), 1) == wanted,
            jnp.broadcast_to(gain[...], (OWN, ALL)),
            0.0,
        ),
        axis=1,
        keepdims=True,
    )
    scale = 1.0 / CELLS

    def summed(group, unit, at):
        _, _, _, _, x_recv, _, _, y_recv, kept = group
        rows = pl.ds(at, 16)
        total = kept[unit, rows, :]
        if unit == 0:
            return total + x_recv[rows, :].astype(F32)
        for slot in range(3):
            total = total + y_recv[slot, rows, :].astype(F32)
        return total

    arrived(first_low)
    arrived(first_high)
    for unit in range(2):
        for at in range(0, RUN, 16):
            line = unit * RUN + at
            gain_rows = gain_own[line : line + 16]
            pre = summed(group_a, unit, at)
            center = pre - jnp.sum(pre, axis=1, keepdims=True) * scale
            inv = lax.rsqrt(jnp.sum(center * center, axis=1, keepdims=True) * scale + NORM_EPS)
            unit_rows = center * inv
            scaled = gain_rows * unit_rows
            sig = jax.nn.sigmoid(scaled)
            normed[pl.ds(line, 16), :] = unit_rows
            sigma[pl.ds(line, 16), :] = sig
            inverse[pl.ds(line, 16), :] = jnp.broadcast_to(inv, (16, 128))
            act[unit, y, x_hi, pl.ds(at, 16), :] = (scaled * sig).astype(BF16)
    act_state = share(act)
    second_low = scatter_on(group_b, 0, second_low)
    second_high = scatter(group_b, 1)
    act_first, act_second = share_on(act, act_state)

    def z_rows(j):
        return pl.ds(pl.multiple_of((z + j) % 4 * ZBLOCK, ZBLOCK), ZBLOCK)

    def lanes(side):
        return pl.ds(pl.multiple_of(side * QUART, QUART), QUART)

    order = (2, 1, 3, 0)

    def reduce_start(columns, gathered, half, unit):
        crossing = {}
        for j in order:
            product[j] = lax.dot_general(
                columns[z_rows(j), :],
                gathered[half].reshape(HALF, CELLS),
                (((1,), (1,)), ((), ())),
                preferred_element_type=F32,
            )
            core_out[unit, j] = product[j, :, lanes(1 - core)].astype(BF16)
            crossing[j] = send(core_out.at[unit, j], core_in.at[unit, j], core_peer)
        z_copies = []
        for j in order:
            crossing[j].wait_recv()
            mine = product[j, :, lanes(core)] + core_in[unit, j].astype(F32)
            if j == 0:
                keep[unit] = mine
            else:
                z_out[unit, j - 1] = mine.astype(BF16)
                z_copies.append(send(z_out.at[unit, j - 1], z_in.at[unit, j - 1], z_peer[j]))
        return z_copies

    def reduce_x(z_copies, unit):
        arrived(z_copies)
        total = keep[unit]
        for slot in range(3):
            total = total + z_in[unit, slot].astype(F32)
        x_out[unit] = total.astype(BF16)
        return send(x_out.at[unit], x_in.at[unit], x_peer)

    factor = 1.0 / math.sqrt(lax.axis_size("dp") * CELLS)

    def spread_z(x_copy, unit, half, final):
        x_copy.wait_recv()
        mine = lanes(half * 2 + core)
        final[z_rows(0), mine] = (
            (x_out[unit].astype(F32) + x_in[unit].astype(F32)) * factor
        ).astype(BF16)
        spot = final.at[z_rows(0), mine]
        copies = {j: send(spot, spot, z_peer[j]) for j in (2, 1, 3)}
        return copies, [send(spot, spot, core_peer)]

    def spread_core(state, half, final):
        to_z, to_core = state
        for j in (1, 3, 2):
            to_z[j].wait_recv()
            spot = final.at[z_rows(4 - j), lanes(half * 2 + core)]
            to_core.append(send(spot, spot, core_peer))
        return to_core

    arrived(act_first)
    z_0 = reduce_start(cot_cols, act, 0, 0)
    second_high = scatter_on(group_b, 1, second_high)
    arrived(act_second)
    z_1 = reduce_start(cot_cols, act, 1, 1)

    arrived(second_low)
    arrived(second_high)
    gain_tile = jnp.zeros((8, 128), F32)
    for unit in range(2):
        for at in range(0, RUN, 16):
            line = unit * RUN + at
            gain_rows = gain_own[line : line + 16]
            dact = summed(group_b, unit, at)
            unit_rows = normed[pl.ds(line, 16), :]
            sig = sigma[pl.ds(line, 16), :]
            inv = inverse[pl.ds(line, 16), 0:1]
            scaled = gain_rows * unit_rows
            dscaled = dact * sig * (1.0 + scaled * (1.0 - sig))
            part = jnp.sum(dscaled * unit_rows, axis=1, keepdims=True)
            first = unit * HALF + chan * RUN + at
            spot = lax.broadcasted_iota(jnp.int32, (16, 128), 1)
            here = lax.broadcasted_iota(jnp.int32, (16, 128), 0) + first % 128
            row = jnp.sum(jnp.where(spot == here, part, 0.0), axis=0, keepdims=True)
            line_at = lax.broadcasted_iota(jnp.int32, (8, 128), 0)
            gain_tile = gain_tile + jnp.where(line_at == first // 128, row, 0.0)
            dnormed = dscaled * gain_rows
            mean_d = jnp.sum(dnormed, axis=1, keepdims=True) * scale
            mean_u = jnp.sum(dnormed * unit_rows, axis=1, keepdims=True) * scale
            back = (dnormed - mean_d - unit_rows * mean_u) * inv
            dpre[unit, y, x_hi, pl.ds(at, 16), :] = back.astype(BF16)
    dpre_state = share(dpre)
    x_0 = reduce_x(z_0, 0)
    dpre_first, dpre_second = share_on(dpre, dpre_state)
    x_1 = reduce_x(z_1, 1)
    gain_all[7] = gain_tile
    gain_copies = [
        send(gain_all.at[7], gain_all.at[slot], device) for slot, (_, device) in enumerate(peers)
    ]
    state_0 = spread_z(x_0, 0, 0, grad_second)
    conv_out(w_second, act, wide, output, 1)
    moves_out = [move(output, output_to)]
    state_1 = spread_z(x_1, 1, 1, grad_second)

    arrived(dpre_first)
    z_2 = reduce_start(vol_cols, dpre, 0, 2)
    last = spread_core(state_0, 0, grad_second)
    arrived(gain_copies)
    total = gain_all[0]
    for slot in range(1, 8):
        total = total + gain_all[slot]
    gain_core[0] = total
    gain_core_copy = send(gain_core.at[0], gain_core.at[1], core_peer)
    arrived(dpre_second)
    z_3 = reduce_start(vol_cols, dpre, 1, 3)
    gain_core_copy.wait_recv()
    gain_z[z] = gain_core[0] + gain_core[1]
    gain_copies = [send(gain_z.at[z], gain_z.at[z], z_peer[j]) for j in (1, 2, 3)]
    x_2 = reduce_x(z_2, 2)
    last += spread_core(state_1, 1, grad_second)
    state_2 = spread_z(x_2, 2, 0, grad_first)
    arrived(gain_copies)
    gain_x[0] = (gain_z[0] + gain_z[1]) + (gain_z[2] + gain_z[3])
    gain_x_copy = send(gain_x.at[0], gain_x.at[1], x_peer)
    x_3 = reduce_x(z_3, 3)
    state_3 = spread_z(x_3, 3, 1, grad_first)
    conv_out(w_first, dpre, wide, grad_volume, -1)
    moves_out.append(move(grad_volume, grad_volume_to))
    gain_x_copy.wait_recv()
    gain_x[2] = (gain_x[0] + gain_x[1]) * factor
    row = jnp.broadcast_to(gain_x[2, pl.ds(chan // 2, 1), :], (8, 128))
    grad_gain[...] = jnp.where(chan % 2 == 0, row, pltpu.roll(row, OWN, axis=1))
    moves_out.append(move(grad_gain, grad_gain_to))
    arrived(last)
    moves_out.append(move(grad_second, grad_second_to))
    final = spread_core(state_2, 0, grad_first)
    final += spread_core(state_3, 1, grad_first)
    for half in range(2):
        arrived(final[4 * half : 4 * half + 4])
        spot = pl.ds(half * HALF, HALF)
        moves_out.append(move(grad_first.at[:, spot], grad_first_to.at[:, spot]))
    for copy in moves_out:
        copy.wait()
    for copy in pending:
        copy.wait_send()


def widen(output, grad_volume, grad_first, grad_gain, grad_second, *results):
    results[0][...] = output[...]
    results[1][...] = grad_volume[...]
    results[2][...] = grad_first[...].astype(F32)
    results[3][...] = grad_gain[0:1, 0:OWN]
    results[4][...] = grad_second[...].astype(F32)


def shards(volume, w_first, gain, w_second, cotangent):
    free = pl.BlockSpec(memory_space=pl.ANY)
    shape = jax.ShapeDtypeStruct
    scattering = [
        pltpu.VMEM((2, 4, 2, RUN, CELLS), BF16),
        pltpu.VMEM((2, 4, 2, RUN, CELLS), F32),
        pltpu.VMEM((3, 2, RUN, CELLS), BF16),
        pltpu.VMEM((RUN, CELLS), BF16),
        pltpu.VMEM((RUN, CELLS), BF16),
        pltpu.VMEM((4, RUN, CELLS), BF16),
        pltpu.VMEM((3, RUN, CELLS), BF16),
        pltpu.VMEM((3, RUN, CELLS), BF16),
        pltpu.VMEM((2, RUN, CELLS), F32),
    ]
    partial = pl.pallas_call(
        kernel,
        name="conv_pair",
        out_shape=(
            shape((OWN, CELLS), BF16),
            shape((OWN, CELLS), BF16),
            shape((TALL, ALL), BF16),
            shape((8, 128), F32),
            shape((TALL, ALL), BF16),
        ),
        in_specs=[free] * 5,
        out_specs=[free] * 5,
        scratch_shapes=[
            pltpu.VMEM((OWN, CELLS), BF16),
            pltpu.VMEM((TALL, ALL), BF16),
            pltpu.VMEM((TALL, ALL), BF16),
            pltpu.VMEM((OWN, CELLS), BF16),
            pltpu.VMEM((OWN, CELLS), BF16),
            pltpu.VMEM((OWN, CELLS), BF16),
            pltpu.VMEM((TALL, ALL), BF16),
            pltpu.VMEM((TALL, ALL), BF16),
            pltpu.VMEM((1, ALL), F32),
            pltpu.VMEM((8, 128), F32),
            pltpu.VMEM((TALL, CELLS), BF16),
            pltpu.VMEM((TALL, CELLS), BF16),
            pltpu.VMEM((ALL, TALL), BF16),
            pltpu.VMEM((2, 4, 2, RUN, CELLS), BF16),
            pltpu.VMEM((2, 4, 2, RUN, CELLS), BF16),
        ]
        + scattering
        + scattering
        + [
            pltpu.VMEM((OWN, CELLS), F32),
            pltpu.VMEM((OWN, CELLS), F32),
            pltpu.VMEM((OWN, 128), F32),
            pltpu.VMEM((9 * OWN, CELLS), F32),
            pltpu.VMEM((4, ZBLOCK, HALF), F32),
            pltpu.VMEM((4, 4, ZBLOCK, QUART), BF16),
            pltpu.VMEM((4, 4, ZBLOCK, QUART), BF16),
            pltpu.VMEM((4, 3, ZBLOCK, QUART), BF16),
            pltpu.VMEM((4, 3, ZBLOCK, QUART), BF16),
            pltpu.VMEM((4, ZBLOCK, QUART), F32),
            pltpu.VMEM((4, ZBLOCK, QUART), BF16),
            pltpu.VMEM((4, ZBLOCK, QUART), BF16),
            pltpu.VMEM((8, 8, 128), F32),
            pltpu.VMEM((2, 8, 128), F32),
            pltpu.VMEM((4, 8, 128), F32),
            pltpu.VMEM((3, 8, 128), F32),
            pltpu.SemaphoreType.DMA((132,)),
            pltpu.SemaphoreType.DMA((132,)),
            pltpu.SemaphoreType.DMA((12,)),
        ],
        compiler_params=pltpu.CompilerParams(
            collective_id=0, has_side_effects=True, vmem_limit_bytes=60 << 20
        ),
    )(
        volume[0],
        w_first.reshape(TALL, ALL),
        gain.reshape(1, ALL),
        w_second.transpose(0, 2, 1).reshape(TALL, ALL),
        cotangent[0],
    )
    small = pl.BlockSpec((OWN // 4, CELLS), lambda i: (i, 0))
    large = pl.BlockSpec((ZBLOCK, ALL), lambda i: (i, 0))
    output, grad_volume, grad_first, grad_gain, grad_second = pl.pallas_call(
        widen,
        name="widen",
        grid=(4,),
        out_shape=(
            shape((OWN, CELLS), BF16),
            shape((OWN, CELLS), BF16),
            shape((TALL, ALL), F32),
            shape((1, OWN), F32),
            shape((TALL, ALL), F32),
        ),
        in_specs=[small, small, large, pl.BlockSpec((8, 128), lambda i: (0, 0)), large],
        out_specs=[small, small, large, pl.BlockSpec((1, OWN), lambda i: (0, 0)), large],
    )(*partial)
    return (
        output[None],
        grad_volume[None],
        grad_first.reshape(TAPS, OWN, ALL),
        grad_gain[0],
        grad_second.reshape(TAPS, OWN, ALL).transpose(0, 2, 1),
    )


def solution(mesh):
    placed = (
        P("dp", "chan", None),
        P(None, "chan", None),
        P(),
        P(None, None, "chan"),
        P("dp", "chan", None),
    )
    return jax.shard_map(
        shards,
        mesh=mesh,
        in_specs=placed,
        out_specs=(
            P("dp", "chan", None),
            P("dp", "chan", None),
            P(None, "chan", None),
            P("chan"),
            P(None, None, "chan"),
        ),
        check_vma=False,
    )
```

```python
import math

import jax
import jax.numpy as jnp
from jax import lax
from jax.experimental import pallas as pl
from jax.experimental.pallas import tpu as pltpu
from jax.sharding import PartitionSpec as P

NORM_EPS = 1e-05
PLANES, ROWS, COLS = 4, 16, 16
PLANE = ROWS * COLS
CELLS = PLANES * PLANE
OWN = 64
ALL = 512
TAPS = 27
TALL = TAPS * OWN
ZBLOCK = TALL // 4
HALF = ALL // 2
QUART = ALL // 4
RUN = 32
MESH = pl.DeviceIdType.MESH
F32 = jnp.float32
BF16 = jnp.bfloat16


def inside(shape, row_off, col_off):
    cell = lax.broadcasted_iota(jnp.int32, shape, 1)
    row = cell // COLS % ROWS + row_off
    col = cell % COLS + col_off
    return (row >= 0) & (row < ROWS) & (col >= 0) & (col < COLS)


def moved(field, row_off, col_off):
    offset = row_off * COLS + col_off
    if offset == 0:
        return field
    rolled = pltpu.roll(field, (-offset) % CELLS, axis=1)
    return jnp.where(inside(field.shape, row_off, col_off), rolled, 0.0)


def build_columns(src, dst, sign):
    field = src[...].astype(F32)
    blank = jnp.zeros((OWN, PLANE), BF16)
    for b in (-1, 0, 1):
        for c in (-1, 0, 1):
            block = moved(field, sign * b, sign * c).astype(BF16)
            for a in (-1, 0, 1):
                tap = 9 * (a + 1) + 3 * (b + 1) + c + 1
                rows = pl.ds(tap * OWN, OWN)
                step = sign * a
                if step == 0:
                    dst[rows, :] = block
                elif step > 0:
                    dst[rows, 0 : CELLS - PLANE] = block[:, PLANE:]
                    dst[rows, CELLS - PLANE : CELLS] = blank
                else:
                    dst[rows, PLANE:CELLS] = block[:, : CELLS - PLANE]
                    dst[rows, 0:PLANE] = blank


def turn(src, dst):
    def one(index, carry):
        at = pl.multiple_of(index * 128, 128)
        dst[:, pl.ds(at, 128)] = src[pl.ds(at, 128), :].T
        return carry

    lax.fori_loop(0, TALL // 128, one, 0)
    rest = TALL // 128 * 128
    dst[:, rest:TALL] = src[rest:TALL, :].T


def partial_sums(turned, columns, wide, dst, first, last):
    def one(index, carry):
        at = pl.multiple_of(index * PLANE, PLANE)
        total = jnp.dot(turned[...], columns[:, pl.ds(at, PLANE)], preferred_element_type=F32)
        total = total.reshape(2, 4, 2, RUN, PLANE)
        wide[:, :, :, :, pl.ds(at, PLANE)] = total
        dst[:, :, :, :, pl.ds(at, PLANE)] = total.astype(BF16)
        return carry

    lax.fori_loop(first, last, one, 0)


def conv_out(weights, gathered, wide, dst, sign):
    nine = 9 * OWN
    for d in range(PLANES):
        total = None
        for a in (-1, 0, 1):
            plane = d + sign * a
            if plane < 0 or plane >= PLANES:
                continue
            term = jnp.dot(
                weights[pl.ds((a + 1) * nine, nine), :],
                gathered[:, :, :, :, pl.ds(plane * PLANE, PLANE)].reshape(ALL, PLANE),
                preferred_element_type=F32,
            )
            total = term if total is None else total + term
        wide[:, pl.ds(d * PLANE, PLANE)] = total

    def one(index, carry):
        at = pl.multiple_of(index * 16, 16)
        total = jnp.zeros((16, CELLS), F32)
        for b in (-1, 0, 1):
            for c in (-1, 0, 1):
                tap = 3 * (b + 1) + c + 1
                total = total + moved(wide[pl.ds(tap * OWN + at, 16), :], sign * b, sign * c)
        dst[pl.ds(at, 16), :] = total.astype(BF16)
        return carry

    lax.fori_loop(0, OWN // 16, one, 0)


def kernel(
    volume_in, w_first_in, gain_in, w_second_in, cotangent_in,
    output, grad_volume, grad_first, grad_gain, grad_second,
    volume, w_first, w_second, cotangent, gain, vol_cols, cot_cols, turned, act, dpre,
    sums_a, wide_a, y_in_a, x_send_a, x_recv_a, x_in_a, y_send_a, y_recv_a, kept_a,
    sums_b, wide_b, y_in_b, x_send_b, x_recv_b, x_in_b, y_send_b, y_recv_b, kept_b,
    normed, sigma, inverse, wide,
    product, core_out, core_in, z_out, z_in, keep, x_out, x_in,
    gain_all, gain_core, gain_z, gain_x, send_sems, recv_sems, own_sems,
):
    dp = lax.axis_index("dp")
    chan = lax.axis_index("chan")
    x_lo, z, core = dp // 8, dp // 2 % 4, dp % 2
    y, x_hi = chan // 2, chan % 2
    pending = []
    moves = []

    def move(src, dst):
        copy = pltpu.make_async_copy(src, dst, own_sems.at[len(moves)])
        copy.start()
        moves.append(copy)
        return copy

    load_volume = move(volume_in, volume)
    load_first = move(w_first_in, w_first)
    load_cotangent = move(cotangent_in, cotangent)
    load_second = move(w_second_in, w_second)
    load_gain = move(gain_in, gain)

    def send(src, dst, device):
        index = len(pending)
        copy = pltpu.make_async_remote_copy(
            src_ref=src,
            dst_ref=dst,
            send_sem=send_sems.at[index],
            recv_sem=recv_sems.at[index],
            device_id=device,
            device_id_type=MESH,
        )
        copy.start()
        pending.append(copy)
        return copy

    peers = []
    for k in (4, 2, 6, 1, 5, 3, 7):
        other = (y + k // 2) % 4 * 2 + (x_hi + k % 2) % 2
        peers.append((other, (dp, other)))
    core_peer = (x_lo * 8 + z * 2 + 1 - core, chan)
    chan_x = (dp, y * 2 + 1 - x_hi)
    chan_y = {j: (dp, (y + j) % 4 * 2 + x_hi) for j in (1, 2, 3)}
    x_peer = ((1 - x_lo) * 8 + z * 2 + core, chan)
    z_peer = {j: (x_lo * 8 + (z + j) % 4 * 2 + core, chan) for j in (1, 2, 3)}

    barrier = pltpu.get_barrier_semaphore()
    everyone = [device for _, device in peers] + [core_peer, x_peer] + list(z_peer.values())
    for device in everyone:
        pl.semaphore_signal(barrier, inc=1, device_id=device, device_id_type=MESH)

    group_a = (sums_a, wide_a, y_in_a, x_send_a, x_recv_a, x_in_a, y_send_a, y_recv_a, kept_a)
    group_b = (sums_b, wide_b, y_in_b, x_send_b, x_recv_b, x_in_b, y_send_b, y_recv_b, kept_b)
    turns = (2, 1, 3)

    def scatter(group, half):
        sums, _, y_in, _, _, x_in, _, _, _ = group
        cells = pl.ds(half * (CELLS // 2), CELLS // 2)
        copies = [send(sums.at[1, :, 1 - x_hi, :, cells], x_in.at[:, :, cells], chan_x)]
        for j in turns:
            spot = sums.at[0, (y + j) % 4, :, :, cells]
            copies.append(send(spot, y_in.at[j - 1, :, :, cells], chan_y[j]))
        return copies

    def scatter_on(group, half, copies):
        _, wide, y_in, x_send, x_recv, x_in, y_send, y_recv, kept = group
        cells = pl.ds(half * (CELLS // 2), CELLS // 2)
        arrived(copies)

        def crossed(side):
            total = wide[0, y, side, :, cells]
            for slot in range(3):
                total = total + y_in[slot, side, :, cells].astype(F32)
            return total

        def along(j):
            row = (y + j) % 4
            return wide[1, row, x_hi, :, cells] + x_in[row, :, cells].astype(F32)

        x_send[:, cells] = crossed(1 - x_hi).astype(BF16)
        later = [send(x_send.at[:, cells], x_recv.at[:, cells], chan_x)]
        for j in turns:
            y_send[j - 1, :, cells] = along(j).astype(BF16)
            later.append(send(y_send.at[j - 1, :, cells], y_recv.at[j - 1, :, cells], chan_y[j]))
        kept[0, :, cells] = crossed(x_hi)
        kept[1, :, cells] = along(0)
        return later

    def share(block):
        own_first = block.at[0, y, x_hi]
        own_second = block.at[1, y, x_hi]
        across = send(own_second, own_second, chan_x)
        along = {j: send(own_first, own_first, chan_y[j]) for j in turns}
        return across, along, [send(own_first, own_first, chan_x)]

    def share_on(block, state):
        across, along, first = state
        across.wait_recv()
        pair = block.at[1, y]
        second = [send(pair, pair, chan_y[j]) for j in turns]
        for j in (1, 3, 2):
            along[j].wait_recv()
            spot = block.at[0, (y + 4 - j) % 4, x_hi]
            first.append(send(spot, spot, chan_x))
        return first, second

    def arrived(copies):
        for copy in copies:
            copy.wait_recv()

    load_volume.wait()
    build_columns(volume, vol_cols, 1)
    load_first.wait()
    turn(w_first, turned)
    partial_sums(turned, vol_cols, wide_a, sums_a, 0, 2)
    pl.semaphore_wait(barrier, len(everyone))
    first_low = scatter(group_a, 0)
    partial_sums(turned, vol_cols, wide_a, sums_a, 2, 4)
    first_high = scatter(group_a, 1)

    load_cotangent.wait()
    build_columns(cotangent, cot_cols, -1)
    load_second.wait()
    turn(w_second, turned)
    first_low = scatter_on(group_a, 0, first_low)
    partial_sums(turned, cot_cols, wide_b, sums_b, 0, 2)
    first_high = scatter_on(group_a, 1, first_high)
    second_low = scatter(group_b, 0)
    partial_sums(turned, cot_cols, wide_b, sums_b, 2, 4)

    load_gain.wait()
    own_row = lax.broadcasted_iota(jnp.int32, (OWN, ALL), 0)
    wanted = own_row // RUN * HALF + chan * RUN + own_row % RUN
    gain_own = jnp.sum(
        jnp.where(
            lax.broadcasted_iota(jnp.int32, (OWN, ALL), 1) == wanted,
            jnp.broadcast_to(gain[...], (OWN, ALL)),
            0.0,
        ),
        axis=1,
        keepdims=True,
    )
    scale = 1.0 / CELLS

    def summed(group, unit, at):
        _, _, _, _, x_recv, _, _, y_recv, kept = group
        rows = pl.ds(at, 16)
        total = kept[unit, rows, :]
        if unit == 0:
            return total + x_recv[rows, :].astype(F32)
        for slot in range(3):
            total = total + y_recv[slot, rows, :].astype(F32)
        return total

    arrived(first_low)
    arrived(first_high)
    for unit in range(2):
        for at in range(0, RUN, 16):
            line = unit * RUN + at
            gain_rows = gain_own[line : line + 16]
            pre = summed(group_a, unit, at)
            center = pre - jnp.sum(pre, axis=1, keepdims=True) * scale
            inv = lax.rsqrt(jnp.sum(center * center, axis=1, keepdims=True) * scale + NORM_EPS)
            unit_rows = center * inv
            scaled = gain_rows * unit_rows
            sig = jax.nn.sigmoid(scaled)
            normed[pl.ds(line, 16), :] = unit_rows
            sigma[pl.ds(line, 16), :] = sig
            inverse[pl.ds(line, 16), :] = jnp.broadcast_to(inv, (16, 128))
            act[unit, y, x_hi, pl.ds(at, 16), :] = (scaled * sig).astype(BF16)
    act_state = share(act)
    second_low = scatter_on(group_b, 0, second_low)
    second_high = scatter(group_b, 1)
    act_first, act_second = share_on(act, act_state)

    def z_rows(j):
        return pl.ds(pl.multiple_of((z + j) % 4 * ZBLOCK, ZBLOCK), ZBLOCK)

    def lanes(side):
        return pl.ds(pl.multiple_of(side * QUART, QUART), QUART)

    order = (2, 1, 3, 0)

    def reduce_start(columns, gathered, half, unit):
        crossing = {}
        for j in order:
            product[j] = lax.dot_general(
                columns[z_rows(j), :],
                gathered[half].reshape(HALF, CELLS),
                (((1,), (1,)), ((), ())),
                preferred_element_type=F32,
            )
            core_out[unit, j] = product[j, :, lanes(1 - core)].astype(BF16)
            crossing[j] = send(core_out.at[unit, j], core_in.at[unit, j], core_peer)
        z_copies = []
        for j in order:
            crossing[j].wait_recv()
            mine = product[j, :, lanes(core)] + core_in[unit, j].astype(F32)
            if j == 0:
                keep[unit] = mine
            else:
                z_out[unit, j - 1] = mine.astype(BF16)
                z_copies.append(send(z_out.at[unit, j - 1], z_in.at[unit, j - 1], z_peer[j]))
        return z_copies

    def reduce_x(z_copies, unit):
        arrived(z_copies)
        total = keep[unit]
        for slot in range(3):
            total = total + z_in[unit, slot].astype(F32)
        x_out[unit] = total.astype(BF16)
        return send(x_out.at[unit], x_in.at[unit], x_peer)

    factor = 1.0 / math.sqrt(lax.axis_size("dp") * CELLS)

    def spread_z(x_copy, unit, half, final):
        x_copy.wait_recv()
        mine = lanes(half * 2 + core)
        final[z_rows(0), mine] = (
            (x_out[unit].astype(F32) + x_in[unit].astype(F32)) * factor
        ).astype(BF16)
        spot = final.at[z_rows(0), mine]
        copies = {j: send(spot, spot, z_peer[j]) for j in (2, 1, 3)}
        return copies, [send(spot, spot, core_peer)]

    def spread_core(state, half, final):
        to_z, to_core = state
        for j in (1, 3, 2):
            to_z[j].wait_recv()
            spot = final.at[z_rows(4 - j), lanes(half * 2 + core)]
            to_core.append(send(spot, spot, core_peer))
        return to_core

    arrived(act_first)
    z_0 = reduce_start(cot_cols, act, 0, 0)
    second_high = scatter_on(group_b, 1, second_high)
    arrived(act_second)
    z_1 = reduce_start(cot_cols, act, 1, 1)

    arrived(second_low)
    arrived(second_high)
    gain_tile = jnp.zeros((8, 128), F32)
    for unit in range(2):
        for at in range(0, RUN, 16):
            line = unit * RUN + at
            gain_rows = gain_own[line : line + 16]
            dact = summed(group_b, unit, at)
            unit_rows = normed[pl.ds(line, 16), :]
            sig = sigma[pl.ds(line, 16), :]
            inv = inverse[pl.ds(line, 16), 0:1]
            scaled = gain_rows * unit_rows
            dscaled = dact * sig * (1.0 + scaled * (1.0 - sig))
            part = jnp.sum(dscaled * unit_rows, axis=1, keepdims=True)
            first = unit * HALF + chan * RUN + at
            spot = lax.broadcasted_iota(jnp.int32, (16, 128), 1)
            here = lax.broadcasted_iota(jnp.int32, (16, 128), 0) + first % 128
            row = jnp.sum(jnp.where(spot == here, part, 0.0), axis=0, keepdims=True)
            line_at = lax.broadcasted_iota(jnp.int32, (8, 128), 0)
            gain_tile = gain_tile + jnp.where(line_at == first // 128, row, 0.0)
            dnormed = dscaled * gain_rows
            mean_d = jnp.sum(dnormed, axis=1, keepdims=True) * scale
            mean_u = jnp.sum(dnormed * unit_rows, axis=1, keepdims=True) * scale
            back = (dnormed - mean_d - unit_rows * mean_u) * inv
            dpre[unit, y, x_hi, pl.ds(at, 16), :] = back.astype(BF16)
    dpre_state = share(dpre)
    x_0 = reduce_x(z_0, 0)
    dpre_first, dpre_second = share_on(dpre, dpre_state)
    x_1 = reduce_x(z_1, 1)
    gain_all[7] = gain_tile
    gain_copies = [
        send(gain_all.at[7], gain_all.at[slot], device) for slot, (_, device) in enumerate(peers)
    ]
    state_0 = spread_z(x_0, 0, 0, grad_second)
    conv_out(w_second, act, wide, output, 1)
    state_1 = spread_z(x_1, 1, 1, grad_second)

    arrived(dpre_first)
    z_2 = reduce_start(vol_cols, dpre, 0, 2)
    last = spread_core(state_0, 0, grad_second)
    arrived(gain_copies)
    total = gain_all[0]
    for slot in range(1, 8):
        total = total + gain_all[slot]
    gain_core[0] = total
    gain_core_copy = send(gain_core.at[0], gain_core.at[1], core_peer)
    arrived(dpre_second)
    z_3 = reduce_start(vol_cols, dpre, 1, 3)
    gain_core_copy.wait_recv()
    gain_z[z] = gain_core[0] + gain_core[1]
    gain_copies = [send(gain_z.at[z], gain_z.at[z], z_peer[j]) for j in (1, 2, 3)]
    x_2 = reduce_x(z_2, 2)
    last += spread_core(state_1, 1, grad_second)
    state_2 = spread_z(x_2, 2, 0, grad_first)
    arrived(gain_copies)
    gain_x[0] = (gain_z[0] + gain_z[1]) + (gain_z[2] + gain_z[3])
    gain_x_copy = send(gain_x.at[0], gain_x.at[1], x_peer)
    x_3 = reduce_x(z_3, 3)
    state_3 = spread_z(x_3, 3, 1, grad_first)
    conv_out(w_first, dpre, wide, grad_volume, -1)
    gain_x_copy.wait_recv()
    gain_x[2] = (gain_x[0] + gain_x[1]) * factor
    row = jnp.broadcast_to(gain_x[2, pl.ds(chan // 2, 1), :], (8, 128))
    grad_gain[...] = jnp.where(chan % 2 == 0, row, pltpu.roll(row, OWN, axis=1))
    arrived(last)
    final = spread_core(state_2, 0, grad_first)
    final += spread_core(state_3, 1, grad_first)
    arrived(final)
    for copy in pending:
        copy.wait_send()


def widen(output, grad_volume, grad_first, grad_gain, grad_second, *results):
    step = pl.program_id(0)
    few = pl.ds(pl.multiple_of(step * (OWN // 4), OWN // 4), OWN // 4)
    many = pl.ds(pl.multiple_of(step * ZBLOCK, ZBLOCK), ZBLOCK)
    results[0][...] = output[few, :]
    results[1][...] = grad_volume[few, :]
    results[2][...] = grad_first[many, :].astype(F32)
    results[3][...] = grad_gain[0:1, 0:OWN]
    results[4][...] = grad_second[many, :].astype(F32)


def shards(volume, w_first, gain, w_second, cotangent):
    free = pl.BlockSpec(memory_space=pl.ANY)
    vmem = pl.BlockSpec(memory_space=pltpu.VMEM)
    shape = jax.ShapeDtypeStruct
    scattering = [
        pltpu.VMEM((2, 4, 2, RUN, CELLS), BF16),
        pltpu.VMEM((2, 4, 2, RUN, CELLS), F32),
        pltpu.VMEM((3, 2, RUN, CELLS), BF16),
        pltpu.VMEM((RUN, CELLS), BF16),
        pltpu.VMEM((RUN, CELLS), BF16),
        pltpu.VMEM((4, RUN, CELLS), BF16),
        pltpu.VMEM((3, RUN, CELLS), BF16),
        pltpu.VMEM((3, RUN, CELLS), BF16),
        pltpu.VMEM((2, RUN, CELLS), F32),
    ]
    partial = pl.pallas_call(
        kernel,
        name="conv_pair",
        out_shape=(
            pltpu.VMEM((OWN, CELLS), BF16),
            pltpu.VMEM((OWN, CELLS), BF16),
            pltpu.VMEM((TALL, ALL), BF16),
            pltpu.VMEM((8, 128), F32),
            pltpu.VMEM((TALL, ALL), BF16),
        ),
        in_specs=[free] * 5,
        out_specs=[vmem] * 5,
        scratch_shapes=[
            pltpu.VMEM((OWN, CELLS), BF16),
            pltpu.VMEM((TALL, ALL), BF16),
            pltpu.VMEM((TALL, ALL), BF16),
            pltpu.VMEM((OWN, CELLS), BF16),
            pltpu.VMEM((1, ALL), F32),
            pltpu.VMEM((TALL, CELLS), BF16),
            pltpu.VMEM((TALL, CELLS), BF16),
            pltpu.VMEM((ALL, TALL), BF16),
            pltpu.VMEM((2, 4, 2, RUN, CELLS), BF16),
            pltpu.VMEM((2, 4, 2, RUN, CELLS), BF16),
        ]
        + scattering
        + scattering
        + [
            pltpu.VMEM((OWN, CELLS), F32),
            pltpu.VMEM((OWN, CELLS), F32),
            pltpu.VMEM((OWN, 128), F32),
            pltpu.VMEM((9 * OWN, CELLS), F32),
            pltpu.VMEM((4, ZBLOCK, HALF), F32),
            pltpu.VMEM((4, 4, ZBLOCK, QUART), BF16),
            pltpu.VMEM((4, 4, ZBLOCK, QUART), BF16),
            pltpu.VMEM((4, 3, ZBLOCK, QUART), BF16),
            pltpu.VMEM((4, 3, ZBLOCK, QUART), BF16),
            pltpu.VMEM((4, ZBLOCK, QUART), F32),
            pltpu.VMEM((4, ZBLOCK, QUART), BF16),
            pltpu.VMEM((4, ZBLOCK, QUART), BF16),
            pltpu.VMEM((8, 8, 128), F32),
            pltpu.VMEM((2, 8, 128), F32),
            pltpu.VMEM((4, 8, 128), F32),
            pltpu.VMEM((3, 8, 128), F32),
            pltpu.SemaphoreType.DMA((132,)),
            pltpu.SemaphoreType.DMA((132,)),
            pltpu.SemaphoreType.DMA((12,)),
        ],
        compiler_params=pltpu.CompilerParams(
            collective_id=0, has_side_effects=True, vmem_limit_bytes=50 << 20
        ),
    )(
        *[
            pltpu.with_memory_space_constraint(value, pltpu.HBM)
            for value in (
                volume[0],
                w_first.reshape(TALL, ALL),
                gain.reshape(1, ALL),
                w_second.transpose(0, 2, 1).reshape(TALL, ALL),
                cotangent[0],
            )
        ]
    )
    small = pl.BlockSpec((OWN // 4, CELLS), lambda i: (i, 0))
    large = pl.BlockSpec((ZBLOCK, ALL), lambda i: (i, 0))
    output, grad_volume, grad_first, grad_gain, grad_second = pl.pallas_call(
        widen,
        name="widen",
        grid=(4,),
        compiler_params=pltpu.CompilerParams(vmem_limit_bytes=16 << 20),
        out_shape=(
            shape((OWN, CELLS), BF16),
            shape((OWN, CELLS), BF16),
            shape((TALL, ALL), F32),
            shape((1, OWN), F32),
            shape((TALL, ALL), F32),
        ),
        in_specs=[vmem] * 5,
        out_specs=[small, small, large, pl.BlockSpec((1, OWN), lambda i: (0, 0)), large],
    )(*[pltpu.with_memory_space_constraint(value, pltpu.VMEM) for value in partial])
    return (
        output[None],
        grad_volume[None],
        grad_first.reshape(TAPS, OWN, ALL),
        grad_gain[0],
        grad_second.reshape(TAPS, OWN, ALL).transpose(0, 2, 1),
    )


def solution(mesh):
    placed = (
        P("dp", "chan", None),
        P(None, "chan", None),
        P(),
        P(None, None, "chan"),
        P("dp", "chan", None),
    )
    return jax.shard_map(
        shards,
        mesh=mesh,
        in_specs=placed,
        out_specs=(
            P("dp", "chan", None),
            P("dp", "chan", None),
            P(None, "chan", None),
            P("chan"),
            P(None, None, "chan"),
        ),
        check_vma=False,
    )
```

```python
import math

import jax
import jax.numpy as jnp
from jax import lax
from jax.experimental import pallas as pl
from jax.experimental.pallas import tpu as pltpu
from jax.sharding import PartitionSpec as P

NORM_EPS = 1e-05
PLANES, ROWS, COLS = 4, 16, 16
PLANE = ROWS * COLS
CELLS = PLANES * PLANE
OWN = 64
ALL = 512
TAPS = 27
TALL = TAPS * OWN
ZBLOCK = TALL // 4
HALF = ALL // 2
QUART = ALL // 4
RUN = 32
MESH = pl.DeviceIdType.MESH
F32 = jnp.float32
BF16 = jnp.bfloat16


def inside(shape, row_off, col_off):
    cell = lax.broadcasted_iota(jnp.int32, shape, 1)
    row = cell // COLS % ROWS + row_off
    col = cell % COLS + col_off
    return (row >= 0) & (row < ROWS) & (col >= 0) & (col < COLS)


def moved(field, row_off, col_off):
    offset = row_off * COLS + col_off
    if offset == 0:
        return field
    rolled = pltpu.roll(field, (-offset) % CELLS, axis=1)
    return jnp.where(inside(field.shape, row_off, col_off), rolled, 0.0)


def build_columns(src, dst, sign):
    field = src[...].astype(F32)
    blank = jnp.zeros((OWN, PLANE), BF16)
    for b in (-1, 0, 1):
        for c in (-1, 0, 1):
            block = moved(field, sign * b, sign * c).astype(BF16)
            for a in (-1, 0, 1):
                tap = 9 * (a + 1) + 3 * (b + 1) + c + 1
                rows = pl.ds(tap * OWN, OWN)
                step = sign * a
                if step == 0:
                    dst[rows, :] = block
                elif step > 0:
                    dst[rows, 0 : CELLS - PLANE] = block[:, PLANE:]
                    dst[rows, CELLS - PLANE : CELLS] = blank
                else:
                    dst[rows, PLANE:CELLS] = block[:, : CELLS - PLANE]
                    dst[rows, 0:PLANE] = blank


def turn(src, dst):
    def one(index, carry):
        at = pl.multiple_of(index * 128, 128)
        dst[:, pl.ds(at, 128)] = src[pl.ds(at, 128), :].T
        return carry

    lax.fori_loop(0, TALL // 128, one, 0)
    rest = TALL // 128 * 128
    dst[:, rest:TALL] = src[rest:TALL, :].T


def partial_sums(turned, columns, wide, dst, first, last):
    def one(index, carry):
        at = pl.multiple_of(index * PLANE, PLANE)
        total = jnp.dot(turned[...], columns[:, pl.ds(at, PLANE)], preferred_element_type=F32)
        total = total.reshape(2, 4, 2, RUN, PLANE)
        wide[:, :, :, :, pl.ds(at, PLANE)] = total
        dst[:, :, :, :, pl.ds(at, PLANE)] = total.astype(BF16)
        return carry

    lax.fori_loop(first, last, one, 0)


def conv_out(weights, gathered, wide, dst, sign):
    nine = 9 * OWN
    for d in range(PLANES):
        total = None
        for a in (-1, 0, 1):
            plane = d + sign * a
            if plane < 0 or plane >= PLANES:
                continue
            term = jnp.dot(
                weights[pl.ds((a + 1) * nine, nine), :],
                gathered[:, :, :, :, pl.ds(plane * PLANE, PLANE)].reshape(ALL, PLANE),
                preferred_element_type=F32,
            )
            total = term if total is None else total + term
        wide[:, pl.ds(d * PLANE, PLANE)] = total

    def one(index, carry):
        at = pl.multiple_of(index * 16, 16)
        total = jnp.zeros((16, CELLS), F32)
        for b in (-1, 0, 1):
            for c in (-1, 0, 1):
                tap = 3 * (b + 1) + c + 1
                total = total + moved(wide[pl.ds(tap * OWN + at, 16), :], sign * b, sign * c)
        dst[pl.ds(at, 16), :] = total.astype(BF16)
        return carry

    lax.fori_loop(0, OWN // 16, one, 0)


def kernel(
    volume_in, w_first_in, gain_in, w_second_in, cotangent_in,
    output, grad_volume, grad_first, grad_gain, grad_second,
    volume, w_first, w_second, cotangent, gain, vol_cols, cot_cols, turned, act, dpre,
    sums_a, wide_a, y_in_a, x_send_a, x_recv_a, x_in_a, y_send_a, y_recv_a, kept_a,
    sums_b, wide_b, y_in_b, x_send_b, x_recv_b, x_in_b, y_send_b, y_recv_b, kept_b,
    normed, sigma, inverse, wide,
    product, core_out, core_in, z_out, z_in, keep, x_out, x_in,
    gain_all, gain_core, gain_z, gain_x, send_sems, recv_sems, own_sems,
):
    dp = lax.axis_index("dp")
    chan = lax.axis_index("chan")
    x_lo, z, core = dp // 8, dp // 2 % 4, dp % 2
    y, x_hi = chan // 2, chan % 2
    pending = []
    moves = []

    def move(src, dst):
        copy = pltpu.make_async_copy(src, dst, own_sems.at[len(moves)])
        copy.start()
        moves.append(copy)
        return copy

    load_volume = move(volume_in, volume)
    load_first = move(w_first_in, w_first)
    load_cotangent = move(cotangent_in, cotangent)
    load_second = move(w_second_in, w_second)
    load_gain = move(gain_in, gain)

    def send(src, dst, device):
        index = len(pending)
        copy = pltpu.make_async_remote_copy(
            src_ref=src,
            dst_ref=dst,
            send_sem=send_sems.at[index],
            recv_sem=recv_sems.at[index],
            device_id=device,
            device_id_type=MESH,
        )
        copy.start()
        pending.append(copy)
        return copy

    peers = []
    for k in (4, 2, 6, 1, 5, 3, 7):
        other = (y + k // 2) % 4 * 2 + (x_hi + k % 2) % 2
        peers.append((other, (dp, other)))
    core_peer = (x_lo * 8 + z * 2 + 1 - core, chan)
    chan_x = (dp, y * 2 + 1 - x_hi)
    chan_y = {j: (dp, (y + j) % 4 * 2 + x_hi) for j in (1, 2, 3)}
    x_peer = ((1 - x_lo) * 8 + z * 2 + core, chan)
    z_peer = {j: (x_lo * 8 + (z + j) % 4 * 2 + core, chan) for j in (1, 2, 3)}

    barrier = pltpu.get_barrier_semaphore()
    everyone = [device for _, device in peers] + [core_peer, x_peer] + list(z_peer.values())
    for device in everyone:
        pl.semaphore_signal(barrier, inc=1, device_id=device, device_id_type=MESH)

    group_a = (sums_a, wide_a, y_in_a, x_send_a, x_recv_a, x_in_a, y_send_a, y_recv_a, kept_a)
    group_b = (sums_b, wide_b, y_in_b, x_send_b, x_recv_b, x_in_b, y_send_b, y_recv_b, kept_b)
    turns = (2, 1, 3)

    def scatter(group, half):
        sums, _, y_in, _, _, x_in, _, _, _ = group
        cells = pl.ds(half * (CELLS // 2), CELLS // 2)
        copies = [send(sums.at[1, :, 1 - x_hi, :, cells], x_in.at[:, :, cells], chan_x)]
        for j in turns:
            spot = sums.at[0, (y + j) % 4, :, :, cells]
            copies.append(send(spot, y_in.at[j - 1, :, :, cells], chan_y[j]))
        return copies

    def scatter_on(group, half, copies):
        _, wide, y_in, x_send, x_recv, x_in, y_send, y_recv, kept = group
        cells = pl.ds(half * (CELLS // 2), CELLS // 2)
        arrived(copies)

        def crossed(side):
            total = wide[0, y, side, :, cells]
            for slot in range(3):
                total = total + y_in[slot, side, :, cells].astype(F32)
            return total

        def along(j):
            row = (y + j) % 4
            return wide[1, row, x_hi, :, cells] + x_in[row, :, cells].astype(F32)

        x_send[:, cells] = crossed(1 - x_hi).astype(BF16)
        later = [send(x_send.at[:, cells], x_recv.at[:, cells], chan_x)]
        for j in turns:
            y_send[j - 1, :, cells] = along(j).astype(BF16)
            later.append(send(y_send.at[j - 1, :, cells], y_recv.at[j - 1, :, cells], chan_y[j]))
        kept[0, :, cells] = crossed(x_hi)
        kept[1, :, cells] = along(0)
        return later

    def share(block):
        own_first = block.at[0, y, x_hi]
        own_second = block.at[1, y, x_hi]
        across = send(own_second, own_second, chan_x)
        along = {j: send(own_first, own_first, chan_y[j]) for j in turns}
        return across, along, [send(own_first, own_first, chan_x)]

    def share_on(block, state):
        across, along, first = state
        across.wait_recv()
        pair = block.at[1, y]
        second = [send(pair, pair, chan_y[j]) for j in turns]
        for j in (1, 3, 2):
            along[j].wait_recv()
            spot = block.at[0, (y + 4 - j) % 4, x_hi]
            first.append(send(spot, spot, chan_x))
        return first, second

    def arrived(copies):
        for copy in copies:
            copy.wait_recv()

    load_volume.wait()
    build_columns(volume, vol_cols, 1)
    load_first.wait()
    turn(w_first, turned)
    partial_sums(turned, vol_cols, wide_a, sums_a, 0, 2)
    pl.semaphore_wait(barrier, len(everyone))
    first_low = scatter(group_a, 0)
    partial_sums(turned, vol_cols, wide_a, sums_a, 2, 4)
    first_high = scatter(group_a, 1)

    load_cotangent.wait()
    build_columns(cotangent, cot_cols, -1)
    load_second.wait()
    turn(w_second, turned)
    first_low = scatter_on(group_a, 0, first_low)
    partial_sums(turned, cot_cols, wide_b, sums_b, 0, 2)
    first_high = scatter_on(group_a, 1, first_high)
    second_low = scatter(group_b, 0)
    partial_sums(turned, cot_cols, wide_b, sums_b, 2, 4)

    load_gain.wait()
    own_row = lax.broadcasted_iota(jnp.int32, (OWN, ALL), 0)
    wanted = own_row // RUN * HALF + chan * RUN + own_row % RUN
    gain_own = jnp.sum(
        jnp.where(
            lax.broadcasted_iota(jnp.int32, (OWN, ALL), 1) == wanted,
            jnp.broadcast_to(gain[...], (OWN, ALL)),
            0.0,
        ),
        axis=1,
        keepdims=True,
    )
    scale = 1.0 / CELLS

    def summed(group, unit, at):
        _, _, _, _, x_recv, _, _, y_recv, kept = group
        rows = pl.ds(at, 16)
        total = kept[unit, rows, :]
        if unit == 0:
            return total + x_recv[rows, :].astype(F32)
        for slot in range(3):
            total = total + y_recv[slot, rows, :].astype(F32)
        return total

    arrived(first_low)
    arrived(first_high)
    for unit in range(2):
        for at in range(0, RUN, 16):
            line = unit * RUN + at
            gain_rows = gain_own[line : line + 16]
            pre = summed(group_a, unit, at)
            center = pre - jnp.sum(pre, axis=1, keepdims=True) * scale
            inv = lax.rsqrt(jnp.sum(center * center, axis=1, keepdims=True) * scale + NORM_EPS)
            unit_rows = center * inv
            scaled = gain_rows * unit_rows
            sig = jax.nn.sigmoid(scaled)
            normed[pl.ds(line, 16), :] = unit_rows
            sigma[pl.ds(line, 16), :] = sig
            inverse[pl.ds(line, 16), :] = jnp.broadcast_to(inv, (16, 128))
            act[unit, y, x_hi, pl.ds(at, 16), :] = (scaled * sig).astype(BF16)
    act_state = share(act)
    second_low = scatter_on(group_b, 0, second_low)
    second_high = scatter(group_b, 1)
    act_first, act_second = share_on(act, act_state)

    def z_rows(j):
        return pl.ds(pl.multiple_of((z + j) % 4 * ZBLOCK, ZBLOCK), ZBLOCK)

    def lanes(side):
        return pl.ds(pl.multiple_of(side * QUART, QUART), QUART)

    order = (1, 3, 2, 0)

    def reduce_start(columns, gathered, half, unit):
        crossing = {}
        for j in order:
            product[j] = lax.dot_general(
                columns[z_rows(j), :],
                gathered[half].reshape(HALF, CELLS),
                (((1,), (1,)), ((), ())),
                preferred_element_type=F32,
            )
            core_out[unit, j] = product[j, :, lanes(1 - core)].astype(BF16)
            crossing[j] = send(core_out.at[unit, j], core_in.at[unit, j], core_peer)
        z_copies = []
        for j in order:
            crossing[j].wait_recv()
            mine = product[j, :, lanes(core)] + core_in[unit, j].astype(F32)
            if j == 0:
                keep[unit] = mine
            else:
                z_out[unit, j - 1] = mine.astype(BF16)
                z_copies.append(send(z_out.at[unit, j - 1], z_in.at[unit, j - 1], z_peer[j]))
        return z_copies

    def reduce_x(z_copies, unit):
        arrived(z_copies)
        total = keep[unit]
        for slot in range(3):
            total = total + z_in[unit, slot].astype(F32)
        x_out[unit] = total.astype(BF16)
        return send(x_out.at[unit], x_in.at[unit], x_peer)

    factor = 1.0 / math.sqrt(lax.axis_size("dp") * CELLS)

    def spread_z(x_copy, unit, half, final):
        x_copy.wait_recv()
        mine = lanes(half * 2 + core)
        final[z_rows(0), mine] = (
            (x_out[unit].astype(F32) + x_in[unit].astype(F32)) * factor
        ).astype(BF16)
        spot = final.at[z_rows(0), mine]
        copies = {j: send(spot, spot, z_peer[j]) for j in (2, 1, 3)}
        return copies, [send(spot, spot, core_peer)]

    def spread_core(state, half, final):
        to_z, to_core = state
        for j in (1, 3, 2):
            to_z[j].wait_recv()
            spot = final.at[z_rows(4 - j), lanes(half * 2 + core)]
            to_core.append(send(spot, spot, core_peer))
        return to_core

    second_high = scatter_on(group_b, 1, second_high)
    arrived(act_first)
    z_0 = reduce_start(cot_cols, act, 0, 0)
    arrived(act_second)
    z_1 = reduce_start(cot_cols, act, 1, 1)

    arrived(second_low)
    arrived(second_high)
    gain_tile = jnp.zeros((8, 128), F32)
    for unit in range(2):
        for at in range(0, RUN, 16):
            line = unit * RUN + at
            gain_rows = gain_own[line : line + 16]
            dact = summed(group_b, unit, at)
            unit_rows = normed[pl.ds(line, 16), :]
            sig = sigma[pl.ds(line, 16), :]
            inv = inverse[pl.ds(line, 16), 0:1]
            scaled = gain_rows * unit_rows
            dscaled = dact * sig * (1.0 + scaled * (1.0 - sig))
            part = jnp.sum(dscaled * unit_rows, axis=1, keepdims=True)
            first = unit * HALF + chan * RUN + at
            spot = lax.broadcasted_iota(jnp.int32, (16, 128), 1)
            here = lax.broadcasted_iota(jnp.int32, (16, 128), 0) + first % 128
            row = jnp.sum(jnp.where(spot == here, part, 0.0), axis=0, keepdims=True)
            line_at = lax.broadcasted_iota(jnp.int32, (8, 128), 0)
            gain_tile = gain_tile + jnp.where(line_at == first // 128, row, 0.0)
            dnormed = dscaled * gain_rows
            mean_d = jnp.sum(dnormed, axis=1, keepdims=True) * scale
            mean_u = jnp.sum(dnormed * unit_rows, axis=1, keepdims=True) * scale
            back = (dnormed - mean_d - unit_rows * mean_u) * inv
            dpre[unit, y, x_hi, pl.ds(at, 16), :] = back.astype(BF16)
    dpre_state = share(dpre)
    x_0 = reduce_x(z_0, 0)
    dpre_first, dpre_second = share_on(dpre, dpre_state)
    x_1 = reduce_x(z_1, 1)
    gain_all[7] = gain_tile
    gain_copies = [
        send(gain_all.at[7], gain_all.at[slot], device) for slot, (_, device) in enumerate(peers)
    ]
    state_0 = spread_z(x_0, 0, 0, grad_second)
    conv_out(w_second, act, wide, output, 1)
    state_1 = spread_z(x_1, 1, 1, grad_second)

    arrived(dpre_first)
    z_2 = reduce_start(vol_cols, dpre, 0, 2)
    last = spread_core(state_0, 0, grad_second)
    arrived(gain_copies)
    total = gain_all[0]
    for slot in range(1, 8):
        total = total + gain_all[slot]
    gain_core[0] = total
    gain_core_copy = send(gain_core.at[0], gain_core.at[1], core_peer)
    arrived(dpre_second)
    z_3 = reduce_start(vol_cols, dpre, 1, 3)
    gain_core_copy.wait_recv()
    gain_z[z] = gain_core[0] + gain_core[1]
    gain_copies = [send(gain_z.at[z], gain_z.at[z], z_peer[j]) for j in (1, 2, 3)]
    x_2 = reduce_x(z_2, 2)
    last += spread_core(state_1, 1, grad_second)
    state_2 = spread_z(x_2, 2, 0, grad_first)
    arrived(gain_copies)
    gain_x[0] = (gain_z[0] + gain_z[1]) + (gain_z[2] + gain_z[3])
    gain_x_copy = send(gain_x.at[0], gain_x.at[1], x_peer)
    x_3 = reduce_x(z_3, 3)
    state_3 = spread_z(x_3, 3, 1, grad_first)
    conv_out(w_first, dpre, wide, grad_volume, -1)
    gain_x_copy.wait_recv()
    gain_x[2] = (gain_x[0] + gain_x[1]) * factor
    row = jnp.broadcast_to(gain_x[2, pl.ds(chan // 2, 1), :], (8, 128))
    grad_gain[...] = jnp.where(chan % 2 == 0, row, pltpu.roll(row, OWN, axis=1))
    arrived(last)
    final = spread_core(state_2, 0, grad_first)
    final += spread_core(state_3, 1, grad_first)
    arrived(final)
    for copy in pending:
        copy.wait_send()


def widen(output, grad_volume, grad_first, grad_gain, grad_second, *results):
    step = pl.program_id(0)
    few = pl.ds(pl.multiple_of(step * (OWN // 4), OWN // 4), OWN // 4)
    many = pl.ds(pl.multiple_of(step * ZBLOCK, ZBLOCK), ZBLOCK)
    results[0][...] = output[few, :]
    results[1][...] = grad_volume[few, :]
    results[2][...] = grad_first[many, :].astype(F32)
    results[3][...] = grad_gain[0:1, 0:OWN]
    results[4][...] = grad_second[many, :].astype(F32)


def shards(volume, w_first, gain, w_second, cotangent):
    free = pl.BlockSpec(memory_space=pl.ANY)
    vmem = pl.BlockSpec(memory_space=pltpu.VMEM)
    shape = jax.ShapeDtypeStruct
    scattering = [
        pltpu.VMEM((2, 4, 2, RUN, CELLS), BF16),
        pltpu.VMEM((2, 4, 2, RUN, CELLS), F32),
        pltpu.VMEM((3, 2, RUN, CELLS), BF16),
        pltpu.VMEM((RUN, CELLS), BF16),
        pltpu.VMEM((RUN, CELLS), BF16),
        pltpu.VMEM((4, RUN, CELLS), BF16),
        pltpu.VMEM((3, RUN, CELLS), BF16),
        pltpu.VMEM((3, RUN, CELLS), BF16),
        pltpu.VMEM((2, RUN, CELLS), F32),
    ]
    partial = pl.pallas_call(
        kernel,
        name="conv_pair",
        out_shape=(
            pltpu.VMEM((OWN, CELLS), BF16),
            pltpu.VMEM((OWN, CELLS), BF16),
            pltpu.VMEM((TALL, ALL), BF16),
            pltpu.VMEM((8, 128), F32),
            pltpu.VMEM((TALL, ALL), BF16),
        ),
        in_specs=[free] * 5,
        out_specs=[vmem] * 5,
        scratch_shapes=[
            pltpu.VMEM((OWN, CELLS), BF16),
            pltpu.VMEM((TALL, ALL), BF16),
            pltpu.VMEM((TALL, ALL), BF16),
            pltpu.VMEM((OWN, CELLS), BF16),
            pltpu.VMEM((1, ALL), F32),
            pltpu.VMEM((TALL, CELLS), BF16),
            pltpu.VMEM((TALL, CELLS), BF16),
            pltpu.VMEM((ALL, TALL), BF16),
            pltpu.VMEM((2, 4, 2, RUN, CELLS), BF16),
            pltpu.VMEM((2, 4, 2, RUN, CELLS), BF16),
        ]
        + scattering
        + scattering
        + [
            pltpu.VMEM((OWN, CELLS), F32),
            pltpu.VMEM((OWN, CELLS), F32),
            pltpu.VMEM((OWN, 128), F32),
            pltpu.VMEM((9 * OWN, CELLS), F32),
            pltpu.VMEM((4, ZBLOCK, HALF), F32),
            pltpu.VMEM((4, 4, ZBLOCK, QUART), BF16),
            pltpu.VMEM((4, 4, ZBLOCK, QUART), BF16),
            pltpu.VMEM((4, 3, ZBLOCK, QUART), BF16),
            pltpu.VMEM((4, 3, ZBLOCK, QUART), BF16),
            pltpu.VMEM((4, ZBLOCK, QUART), F32),
            pltpu.VMEM((4, ZBLOCK, QUART), BF16),
            pltpu.VMEM((4, ZBLOCK, QUART), BF16),
            pltpu.VMEM((8, 8, 128), F32),
            pltpu.VMEM((2, 8, 128), F32),
            pltpu.VMEM((4, 8, 128), F32),
            pltpu.VMEM((3, 8, 128), F32),
            pltpu.SemaphoreType.DMA((132,)),
            pltpu.SemaphoreType.DMA((132,)),
            pltpu.SemaphoreType.DMA((12,)),
        ],
        compiler_params=pltpu.CompilerParams(
            collective_id=0, has_side_effects=True, vmem_limit_bytes=50 << 20
        ),
    )(
        *[
            pltpu.with_memory_space_constraint(value, pltpu.HBM)
            for value in (
                volume[0],
                w_first.reshape(TALL, ALL),
                gain.reshape(1, ALL),
                w_second.transpose(0, 2, 1).reshape(TALL, ALL),
                cotangent[0],
            )
        ]
    )
    small = pl.BlockSpec((OWN // 4, CELLS), lambda i: (i, 0))
    large = pl.BlockSpec((ZBLOCK, ALL), lambda i: (i, 0))
    output, grad_volume, grad_first, grad_gain, grad_second = pl.pallas_call(
        widen,
        name="widen",
        grid=(4,),
        compiler_params=pltpu.CompilerParams(vmem_limit_bytes=16 << 20),
        out_shape=(
            shape((OWN, CELLS), BF16),
            shape((OWN, CELLS), BF16),
            shape((TALL, ALL), F32),
            shape((1, OWN), F32),
            shape((TALL, ALL), F32),
        ),
        in_specs=[vmem] * 5,
        out_specs=[small, small, large, pl.BlockSpec((1, OWN), lambda i: (0, 0)), large],
    )(*[pltpu.with_memory_space_constraint(value, pltpu.VMEM) for value in partial])
    return (
        output[None],
        grad_volume[None],
        grad_first.reshape(TAPS, OWN, ALL),
        grad_gain[0],
        grad_second.reshape(TAPS, OWN, ALL).transpose(0, 2, 1),
    )


def solution(mesh):
    placed = (
        P("dp", "chan", None),
        P(None, "chan", None),
        P(),
        P(None, None, "chan"),
        P("dp", "chan", None),
    )
    return jax.shard_map(
        shards,
        mesh=mesh,
        in_specs=placed,
        out_specs=(
            P("dp", "chan", None),
            P("dp", "chan", None),
            P(None, "chan", None),
            P("chan"),
            P(None, None, "chan"),
        ),
        check_vma=False,
    )
```

```python
import math

import jax
import jax.numpy as jnp
from jax import lax
from jax.experimental import pallas as pl
from jax.experimental.pallas import tpu as pltpu
from jax.sharding import PartitionSpec as P

NORM_EPS = 1e-05
PLANES, ROWS, COLS = 4, 16, 16
PLANE = ROWS * COLS
CELLS = PLANES * PLANE
OWN = 64
ALL = 512
TAPS = 27
TALL = TAPS * OWN
ZBLOCK = TALL // 4
HALF = ALL // 2
QUART = ALL // 4
RUN = 32
MESH = pl.DeviceIdType.MESH
F32 = jnp.float32
BF16 = jnp.bfloat16


def inside(shape, row_off, col_off):
    cell = lax.broadcasted_iota(jnp.int32, shape, 1)
    row = cell // COLS % ROWS + row_off
    col = cell % COLS + col_off
    return (row >= 0) & (row < ROWS) & (col >= 0) & (col < COLS)


def moved(field, row_off, col_off):
    offset = row_off * COLS + col_off
    if offset == 0:
        return field
    rolled = pltpu.roll(field, (-offset) % CELLS, axis=1)
    return jnp.where(inside(field.shape, row_off, col_off), rolled, 0.0)


def build_columns(src, dst, sign):
    field = src[...].astype(F32)
    blank = jnp.zeros((OWN, PLANE), BF16)
    for b in (-1, 0, 1):
        for c in (-1, 0, 1):
            block = moved(field, sign * b, sign * c).astype(BF16)
            for a in (-1, 0, 1):
                tap = 9 * (a + 1) + 3 * (b + 1) + c + 1
                rows = pl.ds(tap * OWN, OWN)
                step = sign * a
                if step == 0:
                    dst[rows, :] = block
                elif step > 0:
                    dst[rows, 0 : CELLS - PLANE] = block[:, PLANE:]
                    dst[rows, CELLS - PLANE : CELLS] = blank
                else:
                    dst[rows, PLANE:CELLS] = block[:, : CELLS - PLANE]
                    dst[rows, 0:PLANE] = blank


def turn(src, dst):
    def one(index, carry):
        at = pl.multiple_of(index * 128, 128)
        dst[:, pl.ds(at, 128)] = src[pl.ds(at, 128), :].T
        return carry

    lax.fori_loop(0, TALL // 128, one, 0)
    rest = TALL // 128 * 128
    dst[:, rest:TALL] = src[rest:TALL, :].T


def partial_sums(turned, columns, wide, dst, first, last):
    def one(index, carry):
        at = pl.multiple_of(index * PLANE, PLANE)
        total = jnp.dot(turned[...], columns[:, pl.ds(at, PLANE)], preferred_element_type=F32)
        total = total.reshape(2, 4, 2, RUN, PLANE)
        wide[:, :, :, :, pl.ds(at, PLANE)] = total
        dst[:, :, :, :, pl.ds(at, PLANE)] = total.astype(BF16)
        return carry

    lax.fori_loop(first, last, one, 0)


def conv_out(weights, gathered, wide, dst, sign):
    nine = 9 * OWN
    for d in range(PLANES):
        total = None
        for a in (-1, 0, 1):
            plane = d + sign * a
            if plane < 0 or plane >= PLANES:
                continue
            term = jnp.dot(
                weights[pl.ds((a + 1) * nine, nine), :],
                gathered[:, :, :, :, pl.ds(plane * PLANE, PLANE)].reshape(ALL, PLANE),
                preferred_element_type=F32,
            )
            total = term if total is None else total + term
        wide[:, pl.ds(d * PLANE, PLANE)] = total

    def one(index, carry):
        at = pl.multiple_of(index * 16, 16)
        total = jnp.zeros((16, CELLS), F32)
        for b in (-1, 0, 1):
            for c in (-1, 0, 1):
                tap = 3 * (b + 1) + c + 1
                total = total + moved(wide[pl.ds(tap * OWN + at, 16), :], sign * b, sign * c)
        dst[pl.ds(at, 16), :] = total.astype(BF16)
        return carry

    lax.fori_loop(0, OWN // 16, one, 0)


def kernel(
    volume_in, w_first_in, gain_in, w_second_in, cotangent_in,
    output, grad_volume, grad_first, grad_gain, grad_second,
    volume, w_first, w_second, cotangent, gain, vol_cols, cot_cols, turned, act, dpre,
    sums_a, wide_a, y_in_a, x_send_a, x_recv_a, x_in_a, y_send_a, y_recv_a, kept_a,
    sums_b, wide_b, y_in_b, x_send_b, x_recv_b, x_in_b, y_send_b, y_recv_b, kept_b,
    normed, sigma, inverse, wide,
    product, core_out, core_in, z_out, z_in, keep, x_out, x_in,
    gain_all, gain_core, gain_z, gain_x, send_sems, recv_sems, own_sems,
):
    dp = lax.axis_index("dp")
    chan = lax.axis_index("chan")
    x_lo, z, core = dp // 8, dp // 2 % 4, dp % 2
    y, x_hi = chan // 2, chan % 2
    pending = []
    moves = []

    def move(src, dst):
        copy = pltpu.make_async_copy(src, dst, own_sems.at[len(moves)])
        copy.start()
        moves.append(copy)
        return copy

    load_volume = move(volume_in, volume)
    load_first = move(w_first_in, w_first)
    load_cotangent = move(cotangent_in, cotangent)
    load_second = move(w_second_in, w_second)
    load_gain = move(gain_in, gain)

    def send(src, dst, device):
        index = len(pending)
        copy = pltpu.make_async_remote_copy(
            src_ref=src,
            dst_ref=dst,
            send_sem=send_sems.at[index],
            recv_sem=recv_sems.at[index],
            device_id=device,
            device_id_type=MESH,
        )
        copy.start()
        pending.append(copy)
        return copy

    peers = []
    for k in (4, 2, 6, 1, 5, 3, 7):
        other = (y + k // 2) % 4 * 2 + (x_hi + k % 2) % 2
        peers.append((other, (dp, other)))
    core_peer = (x_lo * 8 + z * 2 + 1 - core, chan)
    chan_x = (dp, y * 2 + 1 - x_hi)
    chan_y = {j: (dp, (y + j) % 4 * 2 + x_hi) for j in (1, 2, 3)}
    x_peer = ((1 - x_lo) * 8 + z * 2 + core, chan)
    z_peer = {j: (x_lo * 8 + (z + j) % 4 * 2 + core, chan) for j in (1, 2, 3)}

    barrier = pltpu.get_barrier_semaphore()
    everyone = [device for _, device in peers] + [core_peer, x_peer] + list(z_peer.values())
    for device in everyone:
        pl.semaphore_signal(barrier, inc=1, device_id=device, device_id_type=MESH)

    group_a = (sums_a, wide_a, y_in_a, x_send_a, x_recv_a, x_in_a, y_send_a, y_recv_a, kept_a)
    group_b = (sums_b, wide_b, y_in_b, x_send_b, x_recv_b, x_in_b, y_send_b, y_recv_b, kept_b)
    turns = (1, 3, 2)

    def scatter(group, half):
        sums, _, y_in, _, _, x_in, _, _, _ = group
        cells = pl.ds(half * (CELLS // 2), CELLS // 2)
        copies = [send(sums.at[1, :, 1 - x_hi, :, cells], x_in.at[:, :, cells], chan_x)]
        for j in turns:
            spot = sums.at[0, (y + j) % 4, :, :, cells]
            copies.append(send(spot, y_in.at[j - 1, :, :, cells], chan_y[j]))
        return copies

    def scatter_on(group, half, copies):
        _, wide, y_in, x_send, x_recv, x_in, y_send, y_recv, kept = group
        cells = pl.ds(half * (CELLS // 2), CELLS // 2)
        arrived(copies)

        def crossed(side):
            total = wide[0, y, side, :, cells]
            for slot in range(3):
                total = total + y_in[slot, side, :, cells].astype(F32)
            return total

        def along(j):
            row = (y + j) % 4
            return wide[1, row, x_hi, :, cells] + x_in[row, :, cells].astype(F32)

        x_send[:, cells] = crossed(1 - x_hi).astype(BF16)
        later = [send(x_send.at[:, cells], x_recv.at[:, cells], chan_x)]
        for j in turns:
            y_send[j - 1, :, cells] = along(j).astype(BF16)
            later.append(send(y_send.at[j - 1, :, cells], y_recv.at[j - 1, :, cells], chan_y[j]))
        kept[0, :, cells] = crossed(x_hi)
        kept[1, :, cells] = along(0)
        return later

    def share(block):
        own_first = block.at[0, y, x_hi]
        own_second = block.at[1, y, x_hi]
        across = send(own_second, own_second, chan_x)
        along = {j: send(own_first, own_first, chan_y[j]) for j in turns}
        return across, along, [send(own_first, own_first, chan_x)]

    def share_on(block, state):
        across, along, first = state
        across.wait_recv()
        pair = block.at[1, y]
        second = [send(pair, pair, chan_y[j]) for j in turns]
        for j in (1, 3, 2):
            along[j].wait_recv()
            spot = block.at[0, (y + 4 - j) % 4, x_hi]
            first.append(send(spot, spot, chan_x))
        return first, second

    def arrived(copies):
        for copy in copies:
            copy.wait_recv()

    load_volume.wait()
    build_columns(volume, vol_cols, 1)
    load_first.wait()
    turn(w_first, turned)
    partial_sums(turned, vol_cols, wide_a, sums_a, 0, 2)
    pl.semaphore_wait(barrier, len(everyone))
    first_low = scatter(group_a, 0)
    partial_sums(turned, vol_cols, wide_a, sums_a, 2, 4)
    first_high = scatter(group_a, 1)

    load_cotangent.wait()
    build_columns(cotangent, cot_cols, -1)
    load_second.wait()
    turn(w_second, turned)
    first_low = scatter_on(group_a, 0, first_low)
    partial_sums(turned, cot_cols, wide_b, sums_b, 0, 2)
    first_high = scatter_on(group_a, 1, first_high)
    second_low = scatter(group_b, 0)
    partial_sums(turned, cot_cols, wide_b, sums_b, 2, 4)

    load_gain.wait()
    own_row = lax.broadcasted_iota(jnp.int32, (OWN, ALL), 0)
    wanted = own_row // RUN * HALF + chan * RUN + own_row % RUN
    gain_own = jnp.sum(
        jnp.where(
            lax.broadcasted_iota(jnp.int32, (OWN, ALL), 1) == wanted,
            jnp.broadcast_to(gain[...], (OWN, ALL)),
            0.0,
        ),
        axis=1,
        keepdims=True,
    )
    scale = 1.0 / CELLS

    def summed(group, unit, at):
        _, _, _, _, x_recv, _, _, y_recv, kept = group
        rows = pl.ds(at, 16)
        total = kept[unit, rows, :]
        if unit == 0:
            return total + x_recv[rows, :].astype(F32)
        for slot in range(3):
            total = total + y_recv[slot, rows, :].astype(F32)
        return total

    arrived(first_low)
    arrived(first_high)
    for unit in range(2):
        for at in range(0, RUN, 16):
            line = unit * RUN + at
            gain_rows = gain_own[line : line + 16]
            pre = summed(group_a, unit, at)
            center = pre - jnp.sum(pre, axis=1, keepdims=True) * scale
            inv = lax.rsqrt(jnp.sum(center * center, axis=1, keepdims=True) * scale + NORM_EPS)
            unit_rows = center * inv
            scaled = gain_rows * unit_rows
            sig = jax.nn.sigmoid(scaled)
            normed[pl.ds(line, 16), :] = unit_rows
            sigma[pl.ds(line, 16), :] = sig
            inverse[pl.ds(line, 16), :] = jnp.broadcast_to(inv, (16, 128))
            act[unit, y, x_hi, pl.ds(at, 16), :] = (scaled * sig).astype(BF16)
    act_state = share(act)
    second_low = scatter_on(group_b, 0, second_low)
    second_high = scatter(group_b, 1)
    act_first, act_second = share_on(act, act_state)

    def z_rows(j):
        return pl.ds(pl.multiple_of((z + j) % 4 * ZBLOCK, ZBLOCK), ZBLOCK)

    def lanes(side):
        return pl.ds(pl.multiple_of(side * QUART, QUART), QUART)

    order = (1, 3, 2, 0)

    def reduce_start(columns, gathered, half, unit):
        crossing = {}
        for j in order:
            product[j] = lax.dot_general(
                columns[z_rows(j), :],
                gathered[half].reshape(HALF, CELLS),
                (((1,), (1,)), ((), ())),
                preferred_element_type=F32,
            )
            core_out[unit, j] = product[j, :, lanes(1 - core)].astype(BF16)
            crossing[j] = send(core_out.at[unit, j], core_in.at[unit, j], core_peer)
        z_copies = []
        for j in order:
            crossing[j].wait_recv()
            mine = product[j, :, lanes(core)] + core_in[unit, j].astype(F32)
            if j == 0:
                keep[unit] = mine
            else:
                z_out[unit, j - 1] = mine.astype(BF16)
                z_copies.append(send(z_out.at[unit, j - 1], z_in.at[unit, j - 1], z_peer[j]))
        return z_copies

    def reduce_x(z_copies, unit):
        arrived(z_copies)
        total = keep[unit]
        for slot in range(3):
            total = total + z_in[unit, slot].astype(F32)
        x_out[unit] = total.astype(BF16)
        return send(x_out.at[unit], x_in.at[unit], x_peer)

    factor = 1.0 / math.sqrt(lax.axis_size("dp") * CELLS)

    def spread_z(x_copy, unit, half, final):
        x_copy.wait_recv()
        mine = lanes(half * 2 + core)
        final[z_rows(0), mine] = (
            (x_out[unit].astype(F32) + x_in[unit].astype(F32)) * factor
        ).astype(BF16)
        spot = final.at[z_rows(0), mine]
        copies = {j: send(spot, spot, z_peer[j]) for j in (2, 1, 3)}
        return copies, [send(spot, spot, core_peer)]

    def spread_core(state, half, final):
        to_z, to_core = state
        for j in (1, 3, 2):
            to_z[j].wait_recv()
            spot = final.at[z_rows(4 - j), lanes(half * 2 + core)]
            to_core.append(send(spot, spot, core_peer))
        return to_core

    second_high = scatter_on(group_b, 1, second_high)
    arrived(act_first)
    z_0 = reduce_start(cot_cols, act, 0, 0)
    arrived(act_second)
    z_1 = reduce_start(cot_cols, act, 1, 1)

    arrived(second_low)
    arrived(second_high)
    gain_tile = jnp.zeros((8, 128), F32)
    for unit in range(2):
        for at in range(0, RUN, 16):
            line = unit * RUN + at
            gain_rows = gain_own[line : line + 16]
            dact = summed(group_b, unit, at)
            unit_rows = normed[pl.ds(line, 16), :]
            sig = sigma[pl.ds(line, 16), :]
            inv = inverse[pl.ds(line, 16), 0:1]
            scaled = gain_rows * unit_rows
            dscaled = dact * sig * (1.0 + scaled * (1.0 - sig))
            part = jnp.sum(dscaled * unit_rows, axis=1, keepdims=True)
            first = unit * HALF + chan * RUN + at
            spot = lax.broadcasted_iota(jnp.int32, (16, 128), 1)
            here = lax.broadcasted_iota(jnp.int32, (16, 128), 0) + first % 128
            row = jnp.sum(jnp.where(spot == here, part, 0.0), axis=0, keepdims=True)
            line_at = lax.broadcasted_iota(jnp.int32, (8, 128), 0)
            gain_tile = gain_tile + jnp.where(line_at == first // 128, row, 0.0)
            dnormed = dscaled * gain_rows
            mean_d = jnp.sum(dnormed, axis=1, keepdims=True) * scale
            mean_u = jnp.sum(dnormed * unit_rows, axis=1, keepdims=True) * scale
            back = (dnormed - mean_d - unit_rows * mean_u) * inv
            dpre[unit, y, x_hi, pl.ds(at, 16), :] = back.astype(BF16)
    dpre_state = share(dpre)
    x_0 = reduce_x(z_0, 0)
    dpre_first, dpre_second = share_on(dpre, dpre_state)
    x_1 = reduce_x(z_1, 1)
    gain_all[7] = gain_tile
    gain_copies = [
        send(gain_all.at[7], gain_all.at[slot], device) for slot, (_, device) in enumerate(peers)
    ]
    state_0 = spread_z(x_0, 0, 0, grad_second)
    conv_out(w_second, act, wide, output, 1)
    state_1 = spread_z(x_1, 1, 1, grad_second)

    arrived(dpre_first)
    z_2 = reduce_start(vol_cols, dpre, 0, 2)
    last = spread_core(state_0, 0, grad_second)
    arrived(gain_copies)
    total = gain_all[0]
    for slot in range(1, 8):
        total = total + gain_all[slot]
    gain_core[0] = total
    gain_core_copy = send(gain_core.at[0], gain_core.at[1], core_peer)
    arrived(dpre_second)
    z_3 = reduce_start(vol_cols, dpre, 1, 3)
    gain_core_copy.wait_recv()
    gain_z[z] = gain_core[0] + gain_core[1]
    gain_copies = [send(gain_z.at[z], gain_z.at[z], z_peer[j]) for j in (1, 2, 3)]
    x_2 = reduce_x(z_2, 2)
    last += spread_core(state_1, 1, grad_second)
    state_2 = spread_z(x_2, 2, 0, grad_first)
    arrived(gain_copies)
    gain_x[0] = (gain_z[0] + gain_z[1]) + (gain_z[2] + gain_z[3])
    gain_x_copy = send(gain_x.at[0], gain_x.at[1], x_peer)
    x_3 = reduce_x(z_3, 3)
    state_3 = spread_z(x_3, 3, 1, grad_first)
    conv_out(w_first, dpre, wide, grad_volume, -1)
    gain_x_copy.wait_recv()
    gain_x[2] = (gain_x[0] + gain_x[1]) * factor
    row = jnp.broadcast_to(gain_x[2, pl.ds(chan // 2, 1), :], (8, 128))
    grad_gain[...] = jnp.where(chan % 2 == 0, row, pltpu.roll(row, OWN, axis=1))
    arrived(last)
    final = spread_core(state_2, 0, grad_first)
    final += spread_core(state_3, 1, grad_first)
    arrived(final)
    for copy in pending:
        copy.wait_send()


def widen(output, grad_volume, grad_first, grad_gain, grad_second, *results):
    step = pl.program_id(0)
    few = pl.ds(pl.multiple_of(step * (OWN // 4), OWN // 4), OWN // 4)
    many = pl.ds(pl.multiple_of(step * ZBLOCK, ZBLOCK), ZBLOCK)
    results[0][...] = output[few, :]
    results[1][...] = grad_volume[few, :]
    results[2][...] = grad_first[many, :].astype(F32)
    results[3][...] = grad_gain[0:1, 0:OWN]
    results[4][...] = grad_second[many, :].astype(F32)


def shards(volume, w_first, gain, w_second, cotangent):
    free = pl.BlockSpec(memory_space=pl.ANY)
    vmem = pl.BlockSpec(memory_space=pltpu.VMEM)
    shape = jax.ShapeDtypeStruct
    scattering = [
        pltpu.VMEM((2, 4, 2, RUN, CELLS), BF16),
        pltpu.VMEM((2, 4, 2, RUN, CELLS), F32),
        pltpu.VMEM((3, 2, RUN, CELLS), BF16),
        pltpu.VMEM((RUN, CELLS), BF16),
        pltpu.VMEM((RUN, CELLS), BF16),
        pltpu.VMEM((4, RUN, CELLS), BF16),
        pltpu.VMEM((3, RUN, CELLS), BF16),
        pltpu.VMEM((3, RUN, CELLS), BF16),
        pltpu.VMEM((2, RUN, CELLS), F32),
    ]
    partial = pl.pallas_call(
        kernel,
        name="conv_pair",
        out_shape=(
            pltpu.VMEM((OWN, CELLS), BF16),
            pltpu.VMEM((OWN, CELLS), BF16),
            pltpu.VMEM((TALL, ALL), BF16),
            pltpu.VMEM((8, 128), F32),
            pltpu.VMEM((TALL, ALL), BF16),
        ),
        in_specs=[free] * 5,
        out_specs=[vmem] * 5,
        scratch_shapes=[
            pltpu.VMEM((OWN, CELLS), BF16),
            pltpu.VMEM((TALL, ALL), BF16),
            pltpu.VMEM((TALL, ALL), BF16),
            pltpu.VMEM((OWN, CELLS), BF16),
            pltpu.VMEM((1, ALL), F32),
            pltpu.VMEM((TALL, CELLS), BF16),
            pltpu.VMEM((TALL, CELLS), BF16),
            pltpu.VMEM((ALL, TALL), BF16),
            pltpu.VMEM((2, 4, 2, RUN, CELLS), BF16),
            pltpu.VMEM((2, 4, 2, RUN, CELLS), BF16),
        ]
        + scattering
        + scattering
        + [
            pltpu.VMEM((OWN, CELLS), F32),
            pltpu.VMEM((OWN, CELLS), F32),
            pltpu.VMEM((OWN, 128), F32),
            pltpu.VMEM((9 * OWN, CELLS), F32),
            pltpu.VMEM((4, ZBLOCK, HALF), F32),
            pltpu.VMEM((4, 4, ZBLOCK, QUART), BF16),
            pltpu.VMEM((4, 4, ZBLOCK, QUART), BF16),
            pltpu.VMEM((4, 3, ZBLOCK, QUART), BF16),
            pltpu.VMEM((4, 3, ZBLOCK, QUART), BF16),
            pltpu.VMEM((4, ZBLOCK, QUART), F32),
            pltpu.VMEM((4, ZBLOCK, QUART), BF16),
            pltpu.VMEM((4, ZBLOCK, QUART), BF16),
            pltpu.VMEM((8, 8, 128), F32),
            pltpu.VMEM((2, 8, 128), F32),
            pltpu.VMEM((4, 8, 128), F32),
            pltpu.VMEM((3, 8, 128), F32),
            pltpu.SemaphoreType.DMA((132,)),
            pltpu.SemaphoreType.DMA((132,)),
            pltpu.SemaphoreType.DMA((12,)),
        ],
        compiler_params=pltpu.CompilerParams(
            collective_id=0, has_side_effects=True, vmem_limit_bytes=50 << 20
        ),
    )(
        *[
            pltpu.with_memory_space_constraint(value, pltpu.HBM)
            for value in (
                volume[0],
                w_first.reshape(TALL, ALL),
                gain.reshape(1, ALL),
                w_second.transpose(0, 2, 1).reshape(TALL, ALL),
                cotangent[0],
            )
        ]
    )
    small = pl.BlockSpec((OWN // 4, CELLS), lambda i: (i, 0))
    large = pl.BlockSpec((ZBLOCK, ALL), lambda i: (i, 0))
    output, grad_volume, grad_first, grad_gain, grad_second = pl.pallas_call(
        widen,
        name="widen",
        grid=(4,),
        compiler_params=pltpu.CompilerParams(vmem_limit_bytes=16 << 20),
        out_shape=(
            shape((OWN, CELLS), BF16),
            shape((OWN, CELLS), BF16),
            shape((TALL, ALL), F32),
            shape((1, OWN), F32),
            shape((TALL, ALL), F32),
        ),
        in_specs=[vmem] * 5,
        out_specs=[small, small, large, pl.BlockSpec((1, OWN), lambda i: (0, 0)), large],
    )(*[pltpu.with_memory_space_constraint(value, pltpu.VMEM) for value in partial])
    return (
        output[None],
        grad_volume[None],
        grad_first.reshape(TAPS, OWN, ALL),
        grad_gain[0],
        grad_second.reshape(TAPS, OWN, ALL).transpose(0, 2, 1),
    )


def solution(mesh):
    placed = (
        P("dp", "chan", None),
        P(None, "chan", None),
        P(),
        P(None, None, "chan"),
        P("dp", "chan", None),
    )
    return jax.shard_map(
        shards,
        mesh=mesh,
        in_specs=placed,
        out_specs=(
            P("dp", "chan", None),
            P("dp", "chan", None),
            P(None, "chan", None),
            P("chan"),
            P(None, None, "chan"),
        ),
        check_vma=False,
    )
```
